32 devices in a mesh: orient: 4 (over z), dom: 2 (over core), shell: 4 (over y, x).
Axes of the slice: x: 2, y: 2, z: 4, core: 2. Of those that a mesh axis runs over, the one named last changes fastest.
Arguments:
- references: bfloat16 [2048, 2, 4096], P('orient', None, 'shell'), may hold values from -6 to 6
- images: bfloat16 [512, 2, 4096], P(('orient', 'dom'), None, 'shell'), may hold values from -20 to 20
- noise_var: float32 [64], replicated, may hold values from 32 to 128
- shell_of: int32 [4096], P('shell'), may hold values from 0 to 63, never falling along the last dimension, each value on 1 to 128 neighbouring positions
- kept_blocks: int32 [4, 2, 3], P('orient', 'dom'), may hold values from -1 to 3, as said below
Outputs:
- weighted: float32 [2048, 2, 4096], P(('orient', 'dom'), None, 'shell')
- log_norm: float32 [512], P(('orient', 'dom'))
The draws below stay inside these ranges and needn't reach their ends.
Inputs may be any that keep to these rules, and one draw needn't show every extreme that they name: `kept_blocks`: each list holds distinct block numbers first, then -1 entries; the list of orientation block o and group d always starts with o; some list holds 3 blocks.
All inputs are finite; a program needn't handle non-finite values.
Results may differ from the reference program's by a relative error of at most 0.0051.
Values may be sent and summed in bfloat16 or wider, within the bound.
A program may use at most 64 MiB of HBM per device.

```python
import math
import jax
import jax.numpy as jnp
import numpy as np
from jax import lax

K = 4096
SHELLS = 64
OR_DEV = 512
IMG_DEV = 64
SHELL_MOST = 128
OBLK = 4
GROUPS = 2
MOST = 3
ORIENT = 2048
IMAGES = 512


def reference_values(key):
    base_key = jax.random.fold_in(key, 101)
    second = jax.random.fold_in(base_key, 1)
    values = jax.random.normal(second, (ORIENT, 2, K))
    return jnp.clip(values, -6.0, 6.0)


def draw_references(key, part):
    return reference_values(key).astype(jnp.bfloat16)


def draw_images(key, part):
    image_key = jax.random.fold_in(key, 202)
    second = jax.random.fold_in(image_key, 1)
    values = jax.random.normal(second, (IMAGES, 2, K))
    return jnp.clip(values, -20.0, 20.0).astype(jnp.bfloat16)


def draw_kept_blocks(key, part):
    list_key = jax.random.fold_in(key, 303)
    first, second, third = jax.random.split(list_key, 3)
    ranks = jax.random.randint(first, (OBLK, GROUPS, OBLK), 0, 1 << 20) * OBLK + jnp.arange(OBLK, dtype=jnp.int32)[None, None, :]
    itself = jnp.arange(OBLK, dtype=jnp.int32)[:, None, None] == jnp.arange(OBLK, dtype=jnp.int32)[None, None, :]
    ranks = jnp.where(itself, -1, ranks)
    order = jnp.argsort(ranks, axis=-1, stable=True)[:, :, :MOST].astype(jnp.int32)
    counts = jax.random.randint(second, (OBLK, GROUPS), 1, MOST + 1)
    chosen_row = jax.random.randint(third, (), 0, OBLK * GROUPS)
    counts = jnp.where(jnp.arange(OBLK * GROUPS, dtype=jnp.int32).reshape(OBLK, GROUPS) == chosen_row, MOST, counts)
    places = jnp.arange(MOST, dtype=jnp.int32)
    return jnp.where(places[None, None, :] < counts[:, :, None], order, -1).astype(jnp.int32)


def split_up(number_of, total, limit, lean):
    weights = [(1 << 20) // math.isqrt(rank ** lean) + 1 for rank in range(2, number_of + 1)]
    rest, given = total - limit - (number_of - 1), [1] * (number_of - 1)
    while rest > 0:
        free = [i for i in range(number_of - 1) if given[i] < limit]
        whole, budget = sum([weights[i] for i in free]), rest
        for i in free:
            more = min(limit - given[i], max(1, budget * weights[i] // whole), rest)
            given[i] = given[i] + more
            rest = rest - more
    return np.array([limit] + given)


def uneven_parts(key, amount, total, limit, skew):
    if amount == 2:
        one = jax.random.randint(key, (), max(1, total - limit), min(limit, total - 1) + 1)
        return jnp.stack([one, total - one])
    sizes = jnp.asarray(split_up(amount, total, limit, skew), jnp.int32)
    pairs = (amount - 1) // 2
    donor, taker = sizes[1:1 + 2 * pairs:2], sizes[2:2 + 2 * pairs:2]
    slack = jnp.minimum(donor - 1, limit - taker)
    passed = jax.random.randint(jax.random.fold_in(key, 1), (pairs,), 0, 1 << 20) % (slack + 1)
    sizes = sizes.at[1:1 + 2 * pairs:2].set(donor - passed).at[2:2 + 2 * pairs:2].set(taker + passed)
    return sizes[jax.random.permutation(jax.random.fold_in(key, 2), amount)]


def setup_inputs(seed: int = 0) -> dict:
    keys = jax.random.split(jax.random.key(seed), 6)
    return {
        "references": draw_references(jax.random.fold_in(keys[5], 71), 0),
        "images": draw_images(jax.random.fold_in(keys[5], 71), 0),
        "noise_var": jnp.clip(jnp.exp(jax.random.uniform(keys[2], (SHELLS,), jnp.float32, math.log(32.0), math.log(128.0))), 32.0, 128.0),
        "shell_of": jnp.searchsorted(jnp.cumsum(uneven_parts(keys[3], SHELLS, K, SHELL_MOST, 1)), jnp.arange(K), side="right").astype(jnp.int32),
        "kept_blocks": draw_kept_blocks(jax.random.fold_in(keys[5], 71), 0),
    }


floor_value = -1e30


def reference(references, images, noise_var, shell_of, kept_blocks):
    blocks = kept_blocks.shape[0]
    groups = kept_blocks.shape[1]
    coef_weight = 1.0 / noise_var[shell_of]
    scaled = (images.astype(jnp.float32) * coef_weight).astype(jnp.bfloat16)
    scaled_flat = scaled.reshape(IMAGES, 2 * K)
    both_weight = jnp.concatenate([coef_weight, coef_weight])
    found = jnp.any(kept_blocks[:, :, :, None] == jnp.arange(blocks, dtype=jnp.int32)[None, None, None, :], axis=2)
    keep_image = jnp.repeat(jnp.transpose(found, (0, 2, 1)).reshape(blocks, blocks * groups), IMG_DEV, axis=1)
    ref_blocks = references.reshape(blocks, OR_DEV, 2 * K)

    def block_scores(inputs):
        ref_rows, keep_row = inputs
        cross = lax.dot_general(ref_rows, scaled_flat, (((1,), (1,)), ((), ())), preferred_element_type=jnp.float32)
        ref_norm = jnp.sum(both_weight[None, :] * jnp.square(ref_rows.astype(jnp.float32)), axis=1)
        value = cross - 0.5 * ref_norm[:, None]
        return jnp.where(keep_row[None, :], value, floor_value)

    scores = lax.map(block_scores, (ref_blocks, keep_image))
    keep_full = keep_image[:, None, :]
    highest = jnp.max(scores, axis=(0, 1))
    total_mass = jnp.sum(jnp.where(keep_full, jnp.exp(scores - highest[None, None, :]), 0.0), axis=(0, 1))
    log_norm = highest + jnp.log(total_mass)
    posterior = jnp.where(keep_full, jnp.exp(scores - log_norm[None, None, :]), 0.0).astype(jnp.bfloat16)
    images_flat = images.reshape(IMAGES, 2 * K)

    def block_sums(post_rows):
        return jnp.dot(post_rows, images_flat, preferred_element_type=jnp.float32)

    weighted = lax.map(block_sums, posterior).reshape(ORIENT, 2, K)
    return weighted, log_norm
```

```python
import functools
import math

import jax
import jax.numpy as jnp
from jax import lax
from jax.experimental import pallas as pl
from jax.experimental.pallas import tpu as pltpu
from jax.sharding import PartitionSpec as P

floor_value = -1e30
MESH = pl.DeviceIdType.MESH


def kernel(
    sizes, kept_ref, noise_ref, shell_ref, raw_ref, whole_ref, prob_ref, home_ref, keep_ref,
    images, part, accum, logn_ref, refs_ref, turned, stage, img_stage, flat_ref, recvp, ebuf, abuf, erecv, lstat, zstat, w_s, rn_s,
    up_sem, dn_sem, img_sem, dom_send, dom_recv, rs_send, rs_recv,
    st_send, st_recv, e_send, e_recv, z_send, z_recv, out_sem, raw_sem, own_sem,
):
    O, D, S = sizes
    z, d, s = lax.axis_index("orient"), lax.axis_index("dom"), lax.axis_index("shell")
    rows, _, half = raw_ref.shape
    img_rows = whole_ref.shape[0]
    lanes = rows // S
    per = S // D
    most = kept_ref.shape[0]
    owner = s // per
    slot = s % per

    def dev(a, b, c):
        return {"orient": a, "dom": b, "shell": c}

    own = pltpu.make_async_copy(whole_ref, img_stage, own_sem)
    own.start()
    fetch = pltpu.make_async_copy(raw_ref, stage, raw_sem)
    fetch.start()
    barrier = pltpu.get_barrier_semaphore()
    for ok, to in ((z < O - 1, z + 1), (z > 0, z + O - 1)):
        @pl.when(ok)
        def _():
            pl.semaphore_signal(
                barrier, inc=1, device_id=dev(lax.rem(to, O), d, s), device_id_type=MESH)

    for od in range(D):
        for os in range(S):
            if od or os:
                pl.semaphore_signal(
                    barrier, inc=1,
                    device_id=dev(z, lax.rem(d + od, D), lax.rem(s + os, S)),
                    device_id_type=MESH,
                )
    own.wait()
    x = img_stage[...]
    for c in range(2):
        flat_ref[:, c * half:(c + 1) * half] = x[:, c, :]

    def img_ref(c):
        return flat_ref.at[:, c * half:(c + 1) * half]

    near = jnp.where(z < O - 1, 1, 0) + jnp.where(z > 0, 1, 0)
    pl.semaphore_wait(barrier, near + D * S - 1)

    def halves(b, j):
        return lambda c: images.at[b, j, c]

    def up(src, j, c):
        return pltpu.make_async_remote_copy(
            src_ref=src(c), dst_ref=images.at[d, j, c], send_sem=up_sem.at[j, c],
            recv_sem=img_sem.at[j, c],
            device_id=dev(lax.rem(z + 1, O), d, s), device_id_type=MESH)

    def down(src, j, c):
        return pltpu.make_async_remote_copy(
            src_ref=src(c), dst_ref=images.at[d, j, c], send_sem=dn_sem.at[j, c],
            recv_sem=img_sem.at[j, c],
            device_id=dev(lax.rem(z + O - 1, O), d, s), device_id_type=MESH)

    def across(src, od, j, c):
        return pltpu.make_async_remote_copy(
            src_ref=src(c), dst_ref=images.at[d, j, c], send_sem=dom_send.at[od, j, c],
            recv_sem=dom_recv.at[od, j, c],
            device_id=dev(z, lax.rem(d + od, D), s), device_id_type=MESH)

    def scatter(j, o):
        to = lax.rem(s + o, S)
        return pltpu.make_async_remote_copy(
            src_ref=part.at[j, to], dst_ref=recvp.at[j, o], send_sem=rs_send.at[j, o],
            recv_sem=rs_recv.at[j, o], device_id=dev(z, d, to), device_id_type=MESH)

    @pl.when(z < O - 1)
    def _():
        for c in range(2):
            up(img_ref, z, c).start()

    @pl.when(z > 0)
    def _():
        for c in range(2):
            down(img_ref, z, c).start()

    for od in range(1, D):
        for c in range(2):
            across(img_ref, od, z, c).start()

    def keep_copy(src, b, j, c):
        return pltpu.make_async_copy(src(c), keep_ref.at[c, b, j], out_sem.at[b, j, c])

    for c in range(2):
        keep_copy(img_ref, d, z, c).start()

    shell = shell_ref[...]
    noise = jnp.ones(shell.shape, jnp.float32)
    for i in range(noise_ref.shape[0]):
        noise = jnp.where(shell == i, noise_ref[i], noise)
    w = 1.0 / noise
    w_s[...] = w

    def norm_rows(c, carry):
        r0 = pl.multiple_of(c * lanes, lanes)
        x = stage[pl.ds(r0, lanes)]
        refs_ref[pl.ds(r0, lanes), :half] = x[:, 0, :]
        refs_ref[pl.ds(r0, lanes), half:] = x[:, 1, :]
        x0 = refs_ref[pl.ds(r0, lanes), :half].astype(jnp.float32)
        x1 = refs_ref[pl.ds(r0, lanes), half:].astype(jnp.float32)
        y = (x0 * x0 + x1 * x1) * w_s[...]
        acc = y[:, :128]
        for k in range(1, y.shape[1] // 128):
            acc = acc + y[:, k * 128:(k + 1) * 128]
        rn_s[c] = 0.5 * jnp.sum(acc.T, axis=0, keepdims=True)
        return carry

    fetch.wait()
    lax.fori_loop(0, S, norm_rows, 0)

    def cross(src, c):
        scaled = (src(c)[...].astype(jnp.float32) * w_s[...]).astype(jnp.bfloat16)
        return lax.dot_general(
            scaled, refs_ref[:, c * half:(c + 1) * half], (((1,), (1,)), ((), ())),
            preferred_element_type=jnp.float32)

    def finish(full, j):
        for k in range(S):
            part[j, k] = full[:, k * lanes:(k + 1) * lanes] - rn_s[k]
        for o in range(1, S):
            scatter(j, o).start()

    def own_block():
        finish(cross(img_ref, 0) + cross(img_ref, 1), z)

    if O == 1:
        own_block()

    def arrive(block, j, c, hop, onward):
        hop(block, j, c).wait_recv()

        @pl.when(onward)
        def _():
            hop(block, j, c).start()

        for od in range(1, D):
            across(block, od, j, c).start()
        keep_copy(block, d, j, c).start()

    lane = lax.broadcasted_iota(jnp.int32, (img_rows, lanes), 1)

    def reduce_block(j):
        v = part[j, s]
        for o in range(1, S):
            scatter(j, o).wait_recv()
            v = v + recvp[j, o]
        want = jnp.full((img_rows, lanes), j, jnp.int32)
        keep = want == kept_ref[0]
        for k in range(1, most):
            keep = keep | (want == kept_ref[k])
        v = jnp.where(keep, v, floor_value)
        m = jnp.max(v, axis=1, keepdims=True)
        e = jnp.where(keep, jnp.exp(v - m), 0.0)
        total = jnp.sum(e, axis=1, keepdims=True)
        at = pl.ds(pl.multiple_of(j * img_rows, img_rows), img_rows)
        ebuf[at, :] = e.astype(jnp.bfloat16)
        abuf[at, :] = jnp.where(lane == 0, m, total)

    def step(t, carry):
        lo = z - t
        hi = z + t
        for c in range(2):
            @pl.when(lo >= 0)
            def _():
                arrive(halves(d, lo), lo, c, up, z < O - 1)

            @pl.when(hi < O)
            def _():
                arrive(halves(d, hi), hi, c, down, z > 0)

            if c == 0:
                pl.when(t == 1)(own_block)

            for side, j, ok in ((0, lo, lo >= 0), (1, hi, hi < O)):
                @pl.when(ok)
                def _():
                    full = cross(halves(d, j), c)
                    if c == 0:
                        accum[side] = full
                    else:
                        finish(accum[side] + full, j)

            if c == 1:
                @pl.when(lo + 1 >= 0)
                def _():
                    reduce_block(lo + 1)

                @pl.when((hi - 1 < O) & (t > 1))
                def _():
                    reduce_block(hi - 1)

        return carry

    lax.fori_loop(1, O, step, 0)

    @pl.when(z == O - 1)
    def _():
        reduce_block(0)

    @pl.when(z == 0)
    def _():
        reduce_block(O - 1)


    lstat[d, s] = abuf[...].T[:2, :]

    def spread(od, os):
        return pltpu.make_async_remote_copy(
            src_ref=lstat.at[d, s], dst_ref=lstat.at[d, s], send_sem=st_send.at[od, os],
            recv_sem=st_recv.at[od, os],
            device_id=dev(z, lax.rem(d + od, D), lax.rem(s + os, S)), device_id_type=MESH)

    peers = [(od, os) for od in range(D) for os in range(S) if od or os]
    for od, os in peers:
        spread(od, os).start()

    def give(to):
        return pltpu.make_async_remote_copy(
            src_ref=ebuf, dst_ref=erecv.at[d, slot], send_sem=e_send.at[to],
            recv_sem=e_recv.at[d, slot], device_id=dev(z, owner, to), device_id_type=MESH)

    def each_give(act):
        for to in range(S):
            @pl.when((owner != d) | (s != to))
            def _():
                act(give(to))

    each_give(lambda c: c.start())

    @pl.when(owner == d)
    def _():
        erecv[d, slot] = ebuf[...]

    for od, os in peers:
        spread(od, os).wait_recv()
    for b in range(D):
        m = lstat[b, 0, 0:1, :]
        for k in range(1, S):
            m = jnp.maximum(m, lstat[b, k, 0:1, :])
        total = jnp.zeros_like(m)
        for k in range(S):
            total = total + lstat[b, k, 1:2, :] * jnp.exp(lstat[b, k, 0:1, :] - m)
        zstat[z, b, 0:1, :] = m
        zstat[z, b, 1:2, :] = total

    def column(o):
        return pltpu.make_async_remote_copy(
            src_ref=zstat.at[z], dst_ref=zstat.at[z], send_sem=z_send.at[o], recv_sem=z_recv.at[o],
            device_id=dev(lax.rem(z + o, O), d, s), device_id_type=MESH)

    for o in range(1, O):
        column(o).start()
    def dom_wait(j, carry):
        for od in range(1, D):
            b = lax.rem(d + D - od, D)
            for c in range(2):
                across(halves(d, j), od, j, c).wait_recv()
                keep_copy(halves(b, j), b, j, c).start()
        return carry

    lax.fori_loop(0, O, dom_wait, 0)

    for q in range(per):
        for b in range(D):
            @pl.when((d * per + q != s) | (d != b))
            def _():
                pltpu.make_async_remote_copy(
                    src_ref=ebuf, dst_ref=erecv.at[b, q], send_sem=e_send.at[0],
                    recv_sem=e_recv.at[b, q], device_id=dev(z, lax.rem(d + 1, D), s),
                    device_id_type=MESH).wait_recv()
    for q in range(per):
        for b in range(D):
            turned[b, q] = erecv[b, q].astype(jnp.float32).T

    for o in range(1, O):
        column(o).wait_recv()
    for b in range(D):
        m = zstat[0, b, 0:1, :]
        for k in range(1, O):
            m = jnp.maximum(m, zstat[k, b, 0:1, :])
        total = jnp.zeros_like(m)
        for k in range(O):
            total = total + zstat[k, b, 1:2, :] * jnp.exp(zstat[k, b, 0:1, :] - m)
        logn_ref[b:b + 1, :] = m + jnp.log(total)

    home = logn_ref[pl.ds(d, 1), :]
    pick = home[:, :img_rows]
    for j in range(1, O):
        pick = jnp.where(z == j, home[:, j * img_rows:(j + 1) * img_rows], pick)
    home_ref[...] = pick


    depth = O * img_rows
    for q in range(per):
        for b in range(D):
            scale = jnp.exp(lstat[b, d * per + q, 0:1, :] - logn_ref[b:b + 1, :])
            p = (turned[b, q] * scale).astype(jnp.bfloat16)
            prob_ref[q * lanes:(q + 1) * lanes, b * depth:(b + 1) * depth] = p

    @pl.when(z < O - 1)
    def _():
        def done(j, carry):
            @pl.when(j <= z)
            def _():
                for c in range(2):
                    up(img_ref, j, c).wait_send()
            return carry
        lax.fori_loop(0, O, done, 0)

    @pl.when(z > 0)
    def _():
        def done(j, carry):
            @pl.when(j >= z)
            def _():
                for c in range(2):
                    down(img_ref, j, c).wait_send()
            return carry
        lax.fori_loop(0, O, done, 0)

    def sent(j, carry):
        for od in range(1, D):
            for c in range(2):
                across(img_ref, od, j, c).wait_send()
        for b in range(D):
            for c in range(2):
                keep_copy(img_ref, b, j, c).wait()
        for o in range(1, S):
            scatter(j, o).wait_send()
        return carry

    lax.fori_loop(0, O, sent, 0)
    for od, os in peers:
        spread(od, os).wait_send()
    each_give(lambda c: c.wait_send())
    for o in range(1, O):
        column(o).wait_send()


def product(prob_ref, home_ref, images, out_ref, logn_ref, total, out_sem):
    halves, width, wide = 2, images.shape[2], 512

    def put(c, n):
        cols = pl.ds(n * wide, wide)
        return pltpu.make_async_copy(
            total.at[c, :, cols], out_ref.at[:, c, cols], out_sem.at[c, n])

    logn_ref[...] = home_ref[...]
    for c in range(halves):
        for n in range(width // wide):
            cols = slice(n * wide, (n + 1) * wide)
            total[c, :, cols] = jnp.dot(
                prob_ref[...], images[c, :, cols], preferred_element_type=jnp.float32)
            put(c, n).start()
    for c in range(halves):
        for n in range(width // wide):
            put(c, n).wait()


def grant(shapes):
    total = 4 * 1024 * 1024
    for item in shapes:
        if getattr(item, "memory_space", None) == pltpu.VMEM:
            total += math.prod(item.shape) * jnp.dtype(item.dtype).itemsize
    return total


def shards(references, images, noise_var, shell_of, kept_blocks):
    O, D, S = (lax.axis_size(a) for a in ("orient", "dom", "shell"))
    rows = references.shape[0]
    img_rows = images.shape[0]
    local = references.shape[2]
    flat = 2 * local
    lanes = rows // S
    own = rows // D
    columns = O * img_rows
    vmem = pl.BlockSpec(memory_space=pltpu.VMEM)
    smem = pl.BlockSpec(memory_space=pltpu.SMEM)
    sem = pltpu.SemaphoreType.DMA
    f32, bf16 = jnp.float32, jnp.bfloat16
    first = [
        pltpu.VMEM((D, O, 2, img_rows, local), bf16),
        pltpu.VMEM((O, S, img_rows, lanes), f32),
        pltpu.VMEM((2, img_rows, rows), f32),
        pltpu.VMEM((D, columns), f32),
        pltpu.VMEM((rows, flat), bf16),
        pltpu.VMEM((D, S // D, lanes, columns), f32),
        pltpu.VMEM((rows, 2, local), bf16),
        pltpu.VMEM((img_rows, 2, local), bf16),
        pltpu.VMEM((img_rows, flat), bf16),
        pltpu.VMEM((O, S, img_rows, lanes), f32),
        pltpu.VMEM((columns, lanes), bf16),
        pltpu.VMEM((columns, lanes), f32),
        pltpu.VMEM((D, S // D, columns, lanes), bf16),
        pltpu.VMEM((D, S, 2, columns), f32),
        pltpu.VMEM((O, D, 2, columns), f32),
        pltpu.VMEM((1, local), f32),
        pltpu.VMEM((S, 1, lanes), f32),
        sem((O, 2)), sem((O, 2)), sem((O, 2)),
        sem((D, O, 2)), sem((D, O, 2)),
        sem((O, S)), sem((O, S)),
        sem((D, S)), sem((D, S)),
        sem((S,)), sem((D, S // D)),
        sem((O,)), sem((O,)), sem((D, O, 2)), sem, sem,
    ]
    probs, home, kept_images = pl.pallas_call(
        functools.partial(kernel, (O, D, S)),
        name="expectation",
        out_shape=(
            jax.ShapeDtypeStruct((own, D * columns), bf16),
            jax.ShapeDtypeStruct((1, img_rows), f32),
            jax.ShapeDtypeStruct((2, D, O, img_rows, local), bf16),
        ),
        in_specs=[smem, smem, vmem, pl.BlockSpec(memory_space=pltpu.HBM), pl.BlockSpec(memory_space=pltpu.HBM)],
        out_specs=(vmem, vmem, pl.BlockSpec(memory_space=pl.ANY)),
        scratch_shapes=first,
        compiler_params=pltpu.CompilerParams(collective_id=0, has_side_effects=True, vmem_limit_bytes=grant(first)),
    )(
        pltpu.with_memory_space_constraint(kept_blocks.reshape(-1), pltpu.HBM),
        pltpu.with_memory_space_constraint(noise_var, pltpu.HBM),
        pltpu.with_memory_space_constraint(shell_of.reshape(1,-1), pltpu.HBM),
        pltpu.with_memory_space_constraint(references, pltpu.HBM),
        pltpu.with_memory_space_constraint(images, pltpu.HBM),
    )
    depth = D * columns
    second = [
        pltpu.VMEM((2, own, local), f32),
        sem((2, local // 512)),
    ]
    weighted, log_norm = pl.pallas_call(
        product,
        name="product",
        out_shape=(
            jax.ShapeDtypeStruct((own, 2, local), f32),
            jax.ShapeDtypeStruct((1, img_rows), f32),
        ),
        in_specs=[vmem, vmem, vmem],
        out_specs=(pl.BlockSpec(memory_space=pl.ANY), vmem),
        scratch_shapes=second,
        compiler_params=pltpu.CompilerParams(vmem_limit_bytes=grant(second)),
    )(probs, home, kept_images.reshape(2, depth, local))
    return weighted, log_norm.reshape(img_rows)


def solution(mesh):
    placed = (
        P("orient", None, "shell"),
        P(("orient", "dom"), None, "shell"),
        P(),
        P("shell"),
        P("orient", "dom", None),
    )
    return jax.shard_map(
        shards,
        mesh=mesh,
        in_specs=placed,
        out_specs=(P(("orient", "dom"), None, "shell"), P(("orient", "dom"))),
        check_vma=False,
    )
```

```python
import functools
import math

import jax
import jax.numpy as jnp
from jax import lax
from jax.experimental import pallas as pl
from jax.experimental.pallas import tpu as pltpu
from jax.sharding import PartitionSpec as P

floor_value = -1e30
MESH = pl.DeviceIdType.MESH
ahead = 2


def kernel(
    sizes, kept_hbm, noise_hbm, shell_hbm, raw_ref, whole_ref, prob_ref, home_ref, keep_ref,
    images, slots, kout, kin, shift, part, recvp, held, refs_ref, stage, img_stage,
    ebuf, erecv, lstat, zstat, logn, w_s, rn_s, shell_ref, kept_ref, noise_ref, ids,
    up_sem, dn_sem, img_sem, dom_send, dom_recv, rs_send, rs_recv, st_send, st_recv,
    e_send, e_recv, z_send, z_recv, k_send, k_recv, out_sem, in_sem,
):
    O, D, S = sizes
    z, d, s = lax.axis_index("orient"), lax.axis_index("dom"), lax.axis_index("shell")
    rows, _, half = raw_ref.shape
    img_rows = whole_ref.shape[0]
    lanes = rows // S
    per = S // D
    most = kept_ref.shape[0]
    owner = s // per
    slot = s % per
    skip = max(O - most, 0)
    room = O - 1 - skip
    hops = max(O - 2, room)
    pieces, chunks = 8, 8
    hr, qr, pr = img_rows // 2, img_rows // 4, rows // pieces

    def dev(a, b, c):
        return {"orient": a, "dom": b, "shell": c}

    inputs = [
        pltpu.make_async_copy(src, dst, in_sem.at[i])
        for i, (src, dst) in enumerate((
            (whole_ref, img_stage), (raw_ref, stage), (kept_hbm, kept_ref),
            (noise_hbm, noise_ref), (shell_hbm, shell_ref)))
    ]
    for copy in inputs:
        copy.start()
    barrier = pltpu.get_barrier_semaphore()
    for ok, to in ((z < O - 1, z + 1), (z > 0, z + O - 1)):
        @pl.when(ok)
        def _():
            pl.semaphore_signal(
                barrier, inc=1, device_id=dev(lax.rem(to, O), d, s), device_id_type=MESH)

    for od in range(D):
        for os in range(S):
            if od or os:
                pl.semaphore_signal(
                    barrier, inc=1,
                    device_id=dev(z, lax.rem(d + od, D), lax.rem(s + os, S)),
                    device_id_type=MESH,
                )

    def used(p):
        if not skip:
            return p >= 0
        return jnp.logical_not(((z == O - 1) & (p < skip)) | ((z == 0) & (p > room)))

    def has(side, t):
        p = z - t if side == 0 else z + t
        inside = (p >= 0) & (p < O)
        return inside & used(p)

    def on(t, act):
        if isinstance(t, int) and t == 0:
            act(z, 0)
            return
        for side in range(2):
            @pl.when(has(side, t))
            def _():
                act(z - t if side == 0 else z + t, side)

    def piece(n):
        h, c, q = n // 4, (n // 2) % 2, n % 2
        return c, pl.ds(h * hr + q * qr, qr)

    def hop(side, src, p, n):
        c, at = piece(n)
        to = lax.rem(z + 1, O) if side == 0 else lax.rem(z + O - 1, O)
        send = up_sem if side == 0 else dn_sem
        return pltpu.make_async_remote_copy(
            src_ref=src.at[c, at], dst_ref=images.at[d, p, c, at], send_sem=send.at[p],
            recv_sem=img_sem.at[p, n], device_id=dev(to, d, s), device_id_type=MESH)

    def step(side, p, m):
        return p - m if side == 0 else p + m

    def choose(side, k, n):
        c, at = piece(n)
        first = step(side, z, k)
        v = images[d, first, c, at].astype(jnp.float32)
        for m in range(1, skip + 1):
            other = images[d, step(side, first, m), c, at].astype(jnp.float32)
            v = jnp.where(shift[side, k + m] == m, other, v)
        slots[side, k, c, at] = v.astype(jnp.bfloat16)

    def relay(side, t, n):
        p = step(side, z, t)
        edge = O - 1 if side == 0 else 0
        before = O - 2 if side == 0 else 1
        plain = (z != edge) & (z != before) if skip else z != edge

        @pl.when(plain)
        def _():
            hop(side, images.at[d, p], p, n).start()

        if skip and not (isinstance(t, int) and t < skip):
            k = t - skip

            @pl.when((z == before) & (k >= 0) & (k < room))
            def _():
                choose(side, k, n)
                hop(side, slots.at[side, k], step(side, z, k), n).start()

    def serve(t, n):
        def arrived(p, side):
            hop(side, images.at[d, p], p, n).wait_recv()
            relay(side, t, n)
        on(t, arrived)

    def across(od, p):
        return pltpu.make_async_remote_copy(
            src_ref=images.at[d, p], dst_ref=images.at[d, p],
            send_sem=dom_send.at[od - 1, p], recv_sem=dom_recv.at[od - 1, p],
            device_id=dev(z, lax.rem(d + od, D), s), device_id_type=MESH)

    def keep_copy(b, p):
        return pltpu.make_async_copy(images.at[b, p], keep_ref.at[:, b, p], out_sem)

    def landed(p, side):
        for od in range(1, D):
            across(od, p).start()
        keep_copy(d, p).start()

    def scatter(p, h, o):
        to = lax.rem(s + o, S)
        at = pl.ds(h * hr, hr)
        return pltpu.make_async_remote_copy(
            src_ref=part.at[p, to, at], dst_ref=recvp.at[p, o - 1, at], send_sem=rs_send.at[p],
            recv_sem=rs_recv.at[p], device_id=dev(z, d, to), device_id_type=MESH)

    peers = [(od, os) for od in range(D) for os in range(S) if od or os]

    def spread(p, od, os):
        return pltpu.make_async_remote_copy(
            src_ref=lstat.at[d * S + s, p], dst_ref=lstat.at[d * S + s, p],
            send_sem=st_send.at[p], recv_sem=st_recv.at[p],
            device_id=dev(z, lax.rem(d + od, D), lax.rem(s + os, S)), device_id_type=MESH)

    def give(p, to):
        return pltpu.make_async_remote_copy(
            src_ref=ebuf.at[p], dst_ref=erecv.at[d * per + slot, p], send_sem=e_send,
            recv_sem=e_recv, device_id=dev(z, owner, to), device_id_type=MESH)

    def give_all(p, side):
        for to in range(S):
            @pl.when((owner != d) | (s != to))
            def _():
                give(p, to).start()

    def publish(p, m, total, name, e):
        mine = d * S + s
        lstat[mine, p, 0:1, :] = m
        lstat[mine, p, 1:2, :] = total
        lstat[mine, p, 2:3, :] = name
        lstat[mine, p, 3:4, :] = jnp.zeros_like(m)
        ebuf[p] = e
        for od, os in peers:
            spread(p, od, os).start()

        @pl.when(owner == d)
        def _():
            erecv[d * per + slot, p] = e

    def drain(ref, send_sem, recv_sem):
        return pltpu.make_async_remote_copy(
            src_ref=ref, dst_ref=ref, send_sem=send_sem, recv_sem=recv_sem,
            device_id=dev(z, lax.rem(d + 1, D), s), device_id_type=MESH)

    def spread_rows(n):
        r0 = pl.multiple_of(n * pr, pr)
        x = stage[pl.ds(r0, pr)]
        refs_ref[pl.ds(r0, pr), :half] = x[:, 0, :]
        refs_ref[pl.ds(r0, pr), half:] = x[:, 1, :]

    def norm_rows(c):
        at = slice(c * lanes, (c + 1) * lanes)
        x0 = refs_ref[at, :half].astype(jnp.float32)
        x1 = refs_ref[at, half:].astype(jnp.float32)
        y = (x0 * x0 + x1 * x1) * w_s[...]
        acc = y[:, :128]
        for k in range(1, y.shape[1] // 128):
            acc = acc + y[:, k * 128:(k + 1) * 128]
        rn_s[c] = 0.5 * jnp.sum(acc.T, axis=0, keepdims=True)

    def cross(p, c, at):
        scaled = (images[d, p, c, at].astype(jnp.float32) * w_s[...]).astype(jnp.bfloat16)
        return lax.dot_general(
            scaled, refs_ref[:, c * half:(c + 1) * half], (((1,), (1,)), ((), ())),
            preferred_element_type=jnp.float32)

    def finish(full, p, h):
        at = pl.ds(h * hr, hr)
        for k in range(S):
            part[p, k, at] = full[:, k * lanes:(k + 1) * lanes] - rn_s[k]
        for o in range(1, S):
            scatter(p, h, o).start()

    def whole_block(p, side):
        every = slice(0, img_rows)
        full = cross(p, 0, every) + cross(p, 1, every)
        for h in range(2):
            finish(full[h * hr:(h + 1) * hr], p, h)

    def reduce_block(p, side):
        drain(recvp.at[p], rs_send.at[p], rs_recv.at[p]).wait_recv()
        v = part[p, s]
        for o in range(S - 1):
            v = v + recvp[p, o]
        v = v.T
        want = jnp.full(v.shape, ids[p], jnp.int32)
        keep = want == kept_ref[0]
        for k in range(1, most):
            keep = keep | (want == kept_ref[k])
        v = jnp.where(keep, v, floor_value)
        m = jnp.max(v, axis=0, keepdims=True)
        e = jnp.where(keep, jnp.exp(v - m), 0.0)
        total = jnp.sum(e, axis=0, keepdims=True)
        publish(p, m, total, want[:1].astype(jnp.float32), e.astype(jnp.bfloat16))

    inputs[0].wait()
    x = img_stage[...]
    for c in range(2):
        images[d, z, c] = x[:, c, :]
    inputs[2].wait()
    inputs[1].wait()
    for n in range(ahead):
        spread_rows(n)
    near = jnp.where(z < O - 1, 1, 0) + jnp.where(z > 0, 1, 0)
    pl.semaphore_wait(barrier, near + D * S - 1)

    def kept_copy(side):
        to = lax.rem(z + O - 1, O) if side == 0 else lax.rem(z + 1, O)
        return pltpu.make_async_remote_copy(
            src_ref=kout, dst_ref=kin.at[side], send_sem=k_send.at[side],
            recv_sem=k_recv.at[side], device_id=dev(to, d, s), device_id_type=MESH)

    if skip:
        @pl.when((z == 0) | (z == O - 1))
        def _():
            for k in range(most):
                kout[k] = jnp.full((1, half), kept_ref[k], jnp.int32).astype(jnp.float32)
        for side, edge in ((0, O - 1), (1, 0)):
            @pl.when(z == edge)
            def _():
                kept_copy(side).start()

    for n in range(chunks):
        for side in range(2):
            relay(side, 0, n)

    landed(z, 0)

    def candidate(side, c):
        return O - 2 - c if side == 0 else 1 + c

    for p in range(O):
        ids[p] = p
    if skip:
        for side, edge in ((0, O - 1), (1, 0)):
            @pl.when(z == edge)
            def _():
                gone, moved = jnp.int32(0), []
                for c in range(O - 1):
                    moved.append(jnp.minimum(gone, skip))
                    need = kept_ref[0] == candidate(side, c)
                    for k in range(1, most):
                        need = need | (kept_ref[k] == candidate(side, c))
                    gone = gone + jnp.where(need, 0, 1)
                for k in range(room):
                    name = jnp.int32(candidate(side, k))
                    for m in range(1, skip + 1):
                        name = jnp.where(moved[k + m] == m, candidate(side, k + m), name)
                    ids[candidate(side, k)] = name
                for k in range(room, O - 1):
                    p = candidate(side, k)
                    for b in range(D):
                        images[b, p] = jnp.zeros((2, img_rows, half), jnp.bfloat16)
                        keep_copy(b, p).start()
                    publish(
                        p, jnp.full((1, img_rows), floor_value, jnp.float32),
                        jnp.zeros((1, img_rows), jnp.float32),
                        jnp.full((1, img_rows), -2.0, jnp.float32),
                        jnp.zeros((lanes, img_rows), jnp.bfloat16))
                    give_all(p, 0)

    def shifts():
        for side, before in ((0, O - 2), (1, 1)) if skip else ():
            @pl.when(z == before)
            def _():
                kept_copy(side).wait_recv()
                gone = jnp.zeros((1, half), jnp.float32)
                for c in range(O - 1):
                    shift[side, c] = jnp.minimum(gone, skip)
                    need = jnp.zeros((1, half), jnp.float32)
                    for k in range(most):
                        need = jnp.where(kin[side, k] == candidate(side, c), 1.0, need)
                    gone = gone + 1.0 - need

    def weights():
        inputs[3].wait()
        inputs[4].wait()
        shell = shell_ref[...]
        noise = jnp.ones(shell.shape, jnp.float32)
        for i in range(noise_ref.shape[0]):
            noise = jnp.where(shell == i, noise_ref[i], noise)
        w_s[...] = 1.0 / noise

    between = (z > 0) & (z < O - 1)
    edge = jnp.logical_not(between)

    def on_side(side, t, act):
        @pl.when(has(side, t))
        def _():
            act(step(side, z, t), side)

    def reduce_and_give(p, side):
        reduce_block(p, side)
        give_all(p, side)

    def run(t, jobs):
        for n in range(chunks):
            serve(t, n)
            for job in jobs.get(n, ()):
                job()
        on(t, landed)

    @pl.when(edge)
    def _():
        for n in range(ahead, pieces):
            spread_rows(n)
        weights()
        for c in range(S):
            norm_rows(c)
        whole_block(z, 0)
        run(1, {})
        on(1, whole_block)
        reduce_and_give(z, 0)

    @pl.when(between)
    def _():
        for n in range(ahead, ahead + 2):
            spread_rows(n)
        shifts()
        rest = [functools.partial(spread_rows, n) for n in range(ahead + 2, pieces)]
        rest += [weights] + [functools.partial(norm_rows, c) for c in range(S)]
        jobs = {n: [rest[n]] for n in range(4)}
        jobs[4] = rest[4:6]
        jobs[5] = rest[6:]
        jobs[6] = [lambda: whole_block(z, 0)]
        run(1, jobs)

    def middle(t, carry):
        pl.when(edge & (t > 2))(lambda: on(t - 1, whole_block))
        run(t, {
            0: [lambda: pl.when(between)(lambda: on_side(0, t - 1, whole_block))],
            2: [lambda: pl.when(between)(lambda: on_side(1, t - 1, whole_block))],
            4: [lambda: pl.when((t > 2) | between)(lambda: on_side(0, t - 2, reduce_and_give))],
            5: [lambda: pl.when(t > 2)(lambda: on_side(1, t - 2, reduce_and_give))],
        })
        return carry

    lax.fori_loop(2, hops, middle, 0)

    low, high = slice(0, hr), slice(hr, img_rows)

    def first_half(p, side):
        finish(cross(p, 0, low) + cross(p, 1, low), p, 0)

    def third_quarter(p, side):
        held[side] = cross(p, 0, high)

    def last_quarter(p, side):
        finish(held[side] + cross(p, 1, high), p, 1)

    if hops > 2:
        pl.when(edge)(lambda: on(hops - 1, whole_block))
    run(hops, {
        0: [lambda: pl.when(between)(lambda: on_side(0, hops - 1, whole_block))],
        2: [lambda: pl.when(between)(lambda: on_side(1, hops - 1, whole_block))],
        3: [lambda: on(hops, first_half)],
        5: [lambda: on(hops, third_quarter)],
        7: [lambda: on(hops, last_quarter)],
    })
    pl.when(between if hops == 2 else z >= 0)(lambda: on(hops - 2, reduce_and_give))
    on(hops - 1, reduce_block)
    on(hops, reduce_block)
    on(hops - 1, give_all)
    on(hops, give_all)

    def stats(p):
        drain(lstat.at[pl.ds(1, D * S - 1), p], st_send.at[p], st_recv.at[p]).wait_recv()
        for b in range(D):
            m = lstat[b * S, p, 0:1, :]
            for k in range(1, S):
                m = jnp.maximum(m, lstat[b * S + k, p, 0:1, :])
            total = jnp.zeros_like(m)
            for k in range(S):
                total = total + lstat[b * S + k, p, 1:2, :] * jnp.exp(lstat[b * S + k, p, 0:1, :] - m)
            zstat[z, b, 0, pl.ds(p, 1), :] = m
            zstat[z, b, 1, pl.ds(p, 1), :] = total
            zstat[z, b, 2, pl.ds(p, 1), :] = lstat[b * S, p, 2:3, :]

    if O > 8:
        lax.fori_loop(0, O, lambda p, carry: (stats(p), carry)[1], 0)
    else:
        for p in range(O):
            stats(p)

    def column(o):
        return pltpu.make_async_remote_copy(
            src_ref=zstat.at[z], dst_ref=zstat.at[z], send_sem=z_send, recv_sem=z_recv,
            device_id=dev(lax.rem(z + o, O), d, s), device_id_type=MESH)

    for o in range(1, O):
        column(o).start()

    def dom_wait(p, carry):
        @pl.when(used(p))
        def _():
            for od in range(1, D):
                across(od, p).wait_recv()
                keep_copy(lax.rem(d + D - od, D), p).start()
        return carry

    lax.fori_loop(0, O, dom_wait, 0)

    @pl.when(owner == d)
    def _():
        drain(erecv.at[pl.ds(1, S - 1)], e_send, e_recv).wait_recv()

    @pl.when(owner != d)
    def _():
        drain(erecv, e_send, e_recv).wait_recv()

    drain(zstat.at[pl.ds(1, O - 1)], z_send, z_recv).wait_recv()
    for b in range(D):
        m_all, t_all, name = zstat[:, b, 0], zstat[:, b, 1], zstat[:, b, 2]
        for j in range(O):
            mine = name == j
            m = jnp.max(jnp.max(jnp.where(mine, m_all, floor_value), axis=0), axis=0, keepdims=True)
            total = jnp.where(mine, t_all * jnp.exp(jnp.where(mine, m_all - m, 0.0)), 0.0)
            total = jnp.sum(jnp.sum(total, axis=0), axis=0, keepdims=True)
            logn[b, j] = m + jnp.log(total)

    pick = logn[d, 0]
    for j in range(1, O):
        pick = jnp.where(z == j, logn[d, j], pick)
    home_ref[...] = pick

    def posterior(b, q, p):
        k = d * per + q
        name = lstat[b * S + k, p, 2:3, :]
        whole = jnp.zeros_like(name)
        for j in range(max(p - skip, 0), min(p + skip, O - 1) + 1):
            whole = jnp.where(name == j, logn[b, j], whole)
        scale = jnp.exp(lstat[b * S + k, p, 0:1, :] - whole)
        return (erecv[b * per + q, p].astype(jnp.float32) * scale).astype(jnp.bfloat16)

    for q in range(per):
        for b in range(D):
            for p in range(0, O, 2):
                both = [posterior(b, q, i) for i in range(p, min(p + 2, O))]
                at = slice((b * O + p) * img_rows, (b * O + p + len(both)) * img_rows)
                prob_ref[q * lanes:(q + 1) * lanes, at] = jnp.concatenate(both, axis=1)

    def sent(p, carry):
        @pl.when(used(p))
        def _():
            for od in range(1, D):
                across(od, p).wait_send()
            drain(recvp.at[p], rs_send.at[p], rs_recv.at[p]).wait_send()
        drain(lstat.at[pl.ds(1, D * S - 1), p], st_send.at[p], st_recv.at[p]).wait_send()

        for side, edge, before in ((0, O - 1, O - 2), (1, 0, 1)):
            beyond = p <= z if side == 0 else p >= z
            went = (z != edge) & beyond
            if skip:
                near_edge = (z == before) & ((p >= O - 1 - room) if side == 0 else (p <= room))
                went = went & ((z != before) | near_edge)

            @pl.when(went)
            def _():
                sem = up_sem if side == 0 else dn_sem
                drain(images.at[d, p], sem.at[p], img_sem.at[p, 0]).wait_send()
        return carry

    lax.fori_loop(0, O, sent, 0)
    @pl.when(owner == d)
    def _():
        drain(erecv.at[pl.ds(1, S - 1)], e_send, e_recv).wait_send()

    @pl.when(owner != d)
    def _():
        drain(erecv, e_send, e_recv).wait_send()

    drain(zstat.at[pl.ds(1, O - 1)], z_send, z_recv).wait_send()
    pltpu.make_async_copy(keep_ref, keep_ref, out_sem).wait()
    if skip:
        for side, edge in ((0, O - 1), (1, 0)):
            @pl.when(z == edge)
            def _():
                kept_copy(side).wait_send()


def product(prob_ref, home_ref, images, out_ref, logn_ref, total, out_sem):
    halves, width, wide = 2, images.shape[2], 512

    def put(c, n):
        cols = pl.ds(n * wide, wide)
        return pltpu.make_async_copy(
            total.at[c, :, cols], out_ref.at[:, c, cols], out_sem.at[c, n])

    logn_ref[...] = home_ref[...]
    for c in range(halves):
        for n in range(width // wide):
            cols = slice(n * wide, (n + 1) * wide)
            total[c, :, cols] = jnp.dot(
                prob_ref[...], images[c, :, cols], preferred_element_type=jnp.float32)
            put(c, n).start()
    for c in range(halves):
        for n in range(width // wide):
            put(c, n).wait()


def grant(shapes):
    total = 6 * 1024 * 1024
    for item in shapes:
        if getattr(item, "memory_space", None) == pltpu.VMEM:
            size = jnp.dtype(item.dtype).itemsize
            *lead, tall, wide = item.shape
            tall, wide = -(-tall // 8) * 8, -(-wide // 128) * 128
            total += math.prod(lead) * tall * wide * size
    return total


def shards(references, images, noise_var, shell_of, kept_blocks):
    O, D, S = (lax.axis_size(a) for a in ("orient", "dom", "shell"))
    rows = references.shape[0]
    img_rows = images.shape[0]
    local = references.shape[2]
    flat = 2 * local
    lanes = rows // S
    own = rows // D
    columns = O * img_rows
    vmem = pl.BlockSpec(memory_space=pltpu.VMEM)
    sem = pltpu.SemaphoreType.DMA
    f32, bf16 = jnp.float32, jnp.bfloat16
    most = kept_blocks.shape[2]
    skip = max(O - most, 0)
    room = O - 1 - skip
    first = [
        pltpu.VMEM((D, O, 2, img_rows, local), bf16),
        pltpu.VMEM((2, room if skip else 1, 2, img_rows, local), bf16),
        pltpu.VMEM((most, 1, local), f32),
        pltpu.VMEM((2, most, 1, local), f32),
        pltpu.VMEM((2, O, 1, local), f32),
        pltpu.VMEM((O, S, img_rows, lanes), f32),
        pltpu.VMEM((O, S - 1, img_rows, lanes), f32),
        pltpu.VMEM((2, img_rows // 2, rows), f32),
        pltpu.VMEM((rows, flat), bf16),
        pltpu.VMEM((rows, 2, local), bf16),
        pltpu.VMEM((img_rows, 2, local), bf16),
        pltpu.VMEM((O, lanes, img_rows), bf16),
        pltpu.VMEM((S, O, lanes, img_rows), bf16),
        pltpu.VMEM((D * S, O, 4, img_rows), f32),
        pltpu.VMEM((O, D, 3, O, img_rows), f32),
        pltpu.VMEM((D, O, 1, img_rows), f32),
        pltpu.VMEM((1, local), f32),
        pltpu.VMEM((S, 1, lanes), f32),
        pltpu.VMEM((1, local), jnp.int32),
        pltpu.SMEM((most,), jnp.int32),
        pltpu.SMEM(noise_var.shape, f32),
        pltpu.SMEM((O,), jnp.int32),
        sem((O,)), sem((O,)), sem((O, 8)),
        sem((D - 1, O)), sem((D - 1, O)),
        sem((O,)), sem((O,)),
        sem((O,)), sem((O,)),
        sem, sem,
        sem, sem, sem((2,)), sem((2,)),
        sem, sem((5,)),
    ]
    probs, home, kept_images = pl.pallas_call(
        functools.partial(kernel, (O, D, S)),
        name="expectation",
        out_shape=(
            jax.ShapeDtypeStruct((own, D * columns), bf16),
            jax.ShapeDtypeStruct((1, img_rows), f32),
            jax.ShapeDtypeStruct((2, D, O, img_rows, local), bf16),
        ),
        in_specs=[pl.BlockSpec(memory_space=pltpu.HBM)] * 5,
        out_specs=(vmem, vmem, pl.BlockSpec(memory_space=pl.ANY)),
        scratch_shapes=first,
        compiler_params=pltpu.CompilerParams(collective_id=0, has_side_effects=True, vmem_limit_bytes=grant(first)),
    )(
        pltpu.with_memory_space_constraint(kept_blocks.reshape(-1), pltpu.HBM),
        pltpu.with_memory_space_constraint(noise_var, pltpu.HBM),
        pltpu.with_memory_space_constraint(shell_of.reshape(1,-1), pltpu.HBM),
        pltpu.with_memory_space_constraint(references, pltpu.HBM),
        pltpu.with_memory_space_constraint(images, pltpu.HBM),
    )
    depth = D * columns
    second = [
        pltpu.VMEM((2, own, local), f32),
        sem((2, local // 512)),
    ]
    weighted, log_norm = pl.pallas_call(
        product,
        name="product",
        out_shape=(
            jax.ShapeDtypeStruct((own, 2, local), f32),
            jax.ShapeDtypeStruct((1, img_rows), f32),
        ),
        in_specs=[vmem, vmem, vmem],
        out_specs=(pl.BlockSpec(memory_space=pl.ANY), vmem),
        scratch_shapes=second,
        compiler_params=pltpu.CompilerParams(vmem_limit_bytes=grant(second)),
    )(probs, home, kept_images.reshape(2, depth, local))
    return weighted, log_norm.reshape(img_rows)


def solution(mesh):
    placed = (
        P("orient", None, "shell"),
        P(("orient", "dom"), None, "shell"),
        P(),
        P("shell"),
        P("orient", "dom", None),
    )
    return jax.shard_map(
        shards,
        mesh=mesh,
        in_specs=placed,
        out_specs=(P(("orient", "dom"), None, "shell"), P(("orient", "dom"))),
        check_vma=False,
    )
```

```python
import functools
import math

import jax
import jax.numpy as jnp
from jax import lax
from jax.experimental import pallas as pl
from jax.experimental.pallas import tpu as pltpu
from jax.sharding import PartitionSpec as P

floor_value = -1e30
MESH = pl.DeviceIdType.MESH


def farthest(O, most):
    skip = max(O - most, 0)
    room = O - 1 - skip
    hops = max(O - 2, room)
    found = {}
    for y in range(O):
        for p in (y - hops, y + hops):
            off = skip and ((y == O - 1 and p < skip) or (y == 0 and p > room))
            if 0 <= p < O and not off:
                found[y] = p
    return found


def kernel(
    sizes, kept_hbm, noise_hbm, shell_hbm, raw_ref, whole_ref, prob_ref, home_ref, keep_ref,
    images, slots, kout, kin, shift, part, recvp, held, full_held, refs_ref, stage, img_stage,
    ebuf, erecv, lstat, zstat, fstat, logn, w_s, rn_s, shell_ref, kept_ref, noise_ref, ids,
    up_sem, dn_sem, img_sem, dom_send, dom_recv, rs_send, rs_recv, st_send, st_recv,
    e_send, e_recv, z_send, z_recv, k_send, k_recv, f_send, f_recv, out_sem, in_sem,
):
    O, D, S = sizes
    z, d, s = lax.axis_index("orient"), lax.axis_index("dom"), lax.axis_index("shell")
    rows, _, half = raw_ref.shape
    img_rows = whole_ref.shape[0]
    lanes = rows // S
    per = S // D
    most = kept_ref.shape[0]
    owner = s // per
    slot = s % per
    skip = max(O - most, 0)
    room = O - 1 - skip
    hops = max(O - 2, room)
    pieces, chunks = 8, 8
    hr, qr, pr = img_rows // 2, img_rows // 4, rows // pieces

    def dev(a, b, c):
        return {"orient": a, "dom": b, "shell": c}

    inputs = [
        pltpu.make_async_copy(src, dst, in_sem.at[i])
        for i, (src, dst) in enumerate((
            (whole_ref, img_stage), (raw_ref, stage), (kept_hbm, kept_ref),
            (noise_hbm, noise_ref), (shell_hbm, shell_ref)))
    ]
    inputs[0].start()
    inputs[2].start()
    barrier = pltpu.get_barrier_semaphore()
    for ok, to in ((z < O - 1, z + 1), (z > 0, z + O - 1)):
        @pl.when(ok)
        def _():
            pl.semaphore_signal(
                barrier, inc=1, device_id=dev(lax.rem(to, O), d, s), device_id_type=MESH)

    for od in range(D):
        for os in range(S):
            if od or os:
                pl.semaphore_signal(
                    barrier, inc=1,
                    device_id=dev(z, lax.rem(d + od, D), lax.rem(s + os, S)),
                    device_id_type=MESH,
                )

    for i in (1, 3, 4):
        inputs[i].start()

    def used(p):
        if not skip:
            return p >= 0
        return jnp.logical_not(((z == O - 1) & (p < skip)) | ((z == 0) & (p > room)))

    def has(side, t):
        p = z - t if side == 0 else z + t
        inside = (p >= 0) & (p < O)
        return inside & used(p)

    def on(t, act):
        if isinstance(t, int) and t == 0:
            act(z, 0)
            return
        for side in range(2):
            @pl.when(has(side, t))
            def _():
                act(z - t if side == 0 else z + t, side)

    def piece(n):
        h, c, q = n // 4, (n // 2) % 2, n % 2
        return c, pl.ds(h * hr + q * qr, qr)

    def hop(side, src, p, n):
        c, at = piece(n)
        to = lax.rem(z + 1, O) if side == 0 else lax.rem(z + O - 1, O)
        send = up_sem if side == 0 else dn_sem
        return pltpu.make_async_remote_copy(
            src_ref=src.at[c, at], dst_ref=images.at[d, p, c, at], send_sem=send.at[p],
            recv_sem=img_sem.at[p, n], device_id=dev(to, d, s), device_id_type=MESH)

    def step(side, p, m):
        return p - m if side == 0 else p + m

    def choose(side, k, n):
        c, at = piece(n)
        first = step(side, z, k)
        v = images[d, first, c, at].astype(jnp.float32)

        def take(m, v):
            other = images[d, step(side, first, m), c, at].astype(jnp.float32)
            return jnp.where(shift[side, k + m] == m, other, v)

        v = lax.fori_loop(1, skip + 1, take, v, unroll=skip < 3)
        slots[side, k, c, at] = v.astype(jnp.bfloat16)

    def relay(side, t, n):
        p = step(side, z, t)
        edge = O - 1 if side == 0 else 0
        before = O - 2 if side == 0 else 1
        plain = (z != edge) & (z != before) if skip else z != edge

        @pl.when(plain)
        def _():
            hop(side, images.at[d, p], p, n).start()

        if skip and not (isinstance(t, int) and t < skip):
            k = t - skip

            @pl.when((z == before) & (k >= 0) & (k < room))
            def _():
                choose(side, k, n)
                hop(side, slots.at[side, k], step(side, z, k), n).start()

    def serve(t, n):
        def arrived(p, side):
            hop(side, images.at[d, p], p, n).wait_recv()
            relay(side, t, n)
        on(t, arrived)

    def across(od, p):
        return pltpu.make_async_remote_copy(
            src_ref=images.at[d, p], dst_ref=images.at[d, p],
            send_sem=dom_send.at[od - 1, p], recv_sem=dom_recv.at[od - 1, p],
            device_id=dev(z, lax.rem(d + od, D), s), device_id_type=MESH)

    def keep_copy(b, p):
        return pltpu.make_async_copy(images.at[b, p], keep_ref.at[:, b, p], out_sem)

    def landed(p, side):
        for od in range(1, D):
            across(od, p).start()
        keep_copy(d, p).start()

    def scatter(p, h, o):
        to = lax.rem(s + o, S)
        at = pl.ds(h * hr, hr)
        return pltpu.make_async_remote_copy(
            src_ref=part.at[p, to, at], dst_ref=recvp.at[p, o - 1, at], send_sem=rs_send.at[p],
            recv_sem=rs_recv.at[p], device_id=dev(z, d, to), device_id_type=MESH)

    peers = [(od, os) for od in range(D) for os in range(S) if od or os]

    def spread(p, od, os):
        return pltpu.make_async_remote_copy(
            src_ref=lstat.at[d * S + s, p], dst_ref=lstat.at[d * S + s, p],
            send_sem=st_send.at[p], recv_sem=st_recv.at[p],
            device_id=dev(z, lax.rem(d + od, D), lax.rem(s + os, S)), device_id_type=MESH)

    def give(p, to):
        return pltpu.make_async_remote_copy(
            src_ref=ebuf.at[p], dst_ref=erecv.at[d * per + slot, p], send_sem=e_send,
            recv_sem=e_recv, device_id=dev(z, owner, to), device_id_type=MESH)

    def give_all(p, side):
        for to in range(S):
            @pl.when((owner != d) | (s != to))
            def _():
                give(p, to).start()

    last_of = farthest(O, most)
    lasts = list(last_of)
    rank = sum(jnp.where(z == y, i, 0) for i, y in enumerate(lasts))
    member = functools.reduce(jnp.logical_or, [z == y for y in lasts])
    last_here = sum(jnp.where(z == y, p, 0) for y, p in last_of.items())
    last_here = jnp.where(member, last_here, -1)

    def everywhere():
        mine = (rank * D + d) * S + s
        for i in range(O):
            y = jnp.where(z < O // 2, O - 1 - i, i)
            for od, os in peers[::-1] + [(0, 0)]:
                copy = pltpu.make_async_remote_copy(
                    src_ref=fstat.at[mine], dst_ref=fstat.at[mine], send_sem=f_send,
                    recv_sem=f_recv,
                    device_id=dev(y, lax.rem(d + od, D), lax.rem(s + os, S)),
                    device_id_type=MESH)
                if od or os:
                    copy.start()
                else:
                    pl.when(y != z)(copy.start)

    def publish(p, m, total, name, e, last=False):
        mine = (rank * D + d) * S + s if last else d * S + s
        ref = fstat.at[mine] if last else lstat.at[mine, p]
        ref[0:1, :] = m
        ref[1:2, :] = total
        ref[2:3, :] = name
        ref[3:4, :] = jnp.zeros_like(m)
        if last:
            everywhere()
        else:
            for od, os in peers:
                spread(p, od, os).start()
        ebuf[p] = e

        @pl.when(owner == d)
        def _():
            erecv[d * per + slot, p] = e

    def drain(ref, send_sem, recv_sem):
        return pltpu.make_async_remote_copy(
            src_ref=ref, dst_ref=ref, send_sem=send_sem, recv_sem=recv_sem,
            device_id=dev(z, lax.rem(d + 1, D), s), device_id_type=MESH)

    def spread_rows(n):
        r0 = pl.multiple_of(n * pr, pr)
        x = stage[pl.ds(r0, pr)]
        refs_ref[pl.ds(r0, pr), :half] = x[:, 0, :]
        refs_ref[pl.ds(r0, pr), half:] = x[:, 1, :]

    def norm_rows(c):
        at = slice(c * lanes, (c + 1) * lanes)
        x0 = refs_ref[at, :half].astype(jnp.float32)
        x1 = refs_ref[at, half:].astype(jnp.float32)
        y = (x0 * x0 + x1 * x1) * w_s[...]
        acc = y[:, :128]
        for k in range(1, y.shape[1] // 128):
            acc = acc + y[:, k * 128:(k + 1) * 128]
        rn_s[c] = 0.5 * jnp.sum(acc.T, axis=0, keepdims=True)

    def cross(p, c, at):
        scaled = (images[d, p, c, at].astype(jnp.float32) * w_s[...]).astype(jnp.bfloat16)
        return lax.dot_general(
            scaled, refs_ref[:, c * half:(c + 1) * half], (((1,), (1,)), ((), ())),
            preferred_element_type=jnp.float32)

    def finish(full, p, h):
        at = pl.ds(h * hr, hr)
        for k in range(S):
            part[p, k, at] = full[:, k * lanes:(k + 1) * lanes] - rn_s[k]
        for o in sorted(range(1, S), key=lambda o: o % 2 == 0):
            scatter(p, h, o).start()

    def whole_block(p, side):
        every = slice(0, img_rows)
        full = cross(p, 0, every) + cross(p, 1, every)
        for h in range(2):
            finish(full[h * hr:(h + 1) * hr], p, h)

    def reduce_block(p, side, last=False):
        drain(recvp.at[p], rs_send.at[p], rs_recv.at[p]).wait_recv()
        v = part[p, s]
        for o in range(S - 1):
            v = v + recvp[p, o]
        v = v.T
        want = jnp.full(v.shape, ids[p], jnp.int32)
        keep = want == kept_ref[0]
        for k in range(1, most):
            keep = keep | (want == kept_ref[k])
        v = jnp.where(keep, v, floor_value)
        m = jnp.max(v, axis=0, keepdims=True)
        e = jnp.where(keep, jnp.exp(v - m), 0.0)
        total = jnp.sum(e, axis=0, keepdims=True)
        publish(p, m, total, want[:1].astype(jnp.float32), e.astype(jnp.bfloat16), last)

    def kept_copy(side):
        to = lax.rem(z + O - 1, O) if side == 0 else lax.rem(z + 1, O)
        return pltpu.make_async_remote_copy(
            src_ref=kout, dst_ref=kin.at[side], send_sem=k_send.at[side],
            recv_sem=k_recv.at[side], device_id=dev(to, d, s), device_id_type=MESH)

    def own_rows(h):
        at = slice(h * hr, (h + 1) * hr)
        x = img_stage[at]
        for c in range(2):
            images[d, z, c, at] = x[:, c, :]

    between = (z > 0) & (z < O - 1)
    tip = jnp.logical_not(between)
    inputs[2].wait()
    if skip:
        @pl.when(tip)
        def _():
            for k in range(most):
                kout[k] = jnp.full((1, 128), kept_ref[k], jnp.int32).astype(jnp.float32)
    inputs[0].wait()
    own_rows(0)
    near = jnp.where(z < O - 1, 1, 0) + jnp.where(z > 0, 1, 0)
    pl.semaphore_wait(barrier, near + D * S - 1)
    if skip:
        for side, last in ((0, O - 1), (1, 0)):
            @pl.when(z == last)
            def _():
                kept_copy(side).start()
    for h in range(2):
        if h:
            own_rows(h)
        for n in range(4 * h, 4 * h + 4):
            for side in range(2):
                relay(side, 0, n)
    landed(z, 0)
    inputs[1].wait()

    def candidate(side, c):
        return O - 2 - c if side == 0 else 1 + c

    for p in range(O):
        ids[p] = p
    if skip:
        for side, edge in ((0, O - 1), (1, 0)):
            @pl.when(z == edge)
            def _():
                gone, moved = jnp.int32(0), []
                for c in range(O - 1):
                    moved.append(jnp.minimum(gone, skip))
                    need = kept_ref[0] == candidate(side, c)
                    for k in range(1, most):
                        need = need | (kept_ref[k] == candidate(side, c))
                    gone = gone + jnp.where(need, 0, 1)
                for k in range(room):
                    name = jnp.int32(candidate(side, k))
                    for m in range(1, skip + 1):
                        name = jnp.where(moved[k + m] == m, candidate(side, k + m), name)
                    ids[candidate(side, k)] = name
                for k in range(room, O - 1):
                    p = candidate(side, k)
                    for b in range(D):
                        images[b, p] = jnp.zeros((2, img_rows, half), jnp.bfloat16)
                        keep_copy(b, p).start()
                    publish(
                        p, jnp.full((1, img_rows), floor_value, jnp.float32),
                        jnp.zeros((1, img_rows), jnp.float32),
                        jnp.full((1, img_rows), -2.0, jnp.float32),
                        jnp.zeros((lanes, img_rows), jnp.bfloat16))
                    give_all(p, 0)

    def shifts():
        for side, before in ((0, O - 2), (1, 1)) if skip else ():
            @pl.when(z == before)
            def _():
                kept_copy(side).wait_recv()
                gone = jnp.zeros((1, 128), jnp.float32)
                for c in range(O - 1):
                    moved = jnp.minimum(gone, skip)
                    shift[side, c] = jnp.concatenate([moved] * (half // 128), axis=1)
                    need = jnp.zeros((1, 128), jnp.float32)
                    for k in range(most):
                        need = jnp.where(kin[side, k] == candidate(side, c), 1.0, need)
                    gone = gone + 1.0 - need

    def weights():
        inputs[3].wait()
        inputs[4].wait()
        shell = shell_ref[...]
        noise = jnp.ones(shell.shape, jnp.float32)
        for i in range(noise_ref.shape[0]):
            noise = jnp.where(shell == i, noise_ref[i], noise)
        w_s[...] = 1.0 / noise

    def on_side(side, t, act):
        @pl.when(has(side, t))
        def _():
            act(step(side, z, t), side)

    def reduce_and_give(p, side):
        reduce_block(p, side)
        give_all(p, side)

    def run(t, jobs):
        for n in range(chunks):
            serve(t, n)
            for job in jobs.get(n, ()):
                job()

    @pl.when(tip)
    def _():
        for n in range(pieces):
            spread_rows(n)
        weights()
        for c in range(S):
            norm_rows(c)
        whole_block(z, 0)
        run(1, {})
        on(1, whole_block)
        on(1, landed)
        reduce_and_give(z, 0)

    @pl.when(between)
    def _():
        for n in range(3):
            spread_rows(n)
        shifts()
        jobs = {n: [functools.partial(spread_rows, n + 3)] for n in range(pieces - 3)}
        norms = [functools.partial(norm_rows, c) for c in range(S)]
        jobs[5] = [weights] + norms[:S // 2]
        jobs[6] = norms[S // 2:]
        run(1, jobs)
        on(1, landed)

    def middle(t, carry):
        pl.when(tip & (t > 2))(lambda: on(t - 1, whole_block))
        pl.when(between & (t == 2))(lambda: whole_block(z, 0))
        run(t, {
            0: [lambda: pl.when(between)(lambda: on_side(0, t - 1, whole_block))],
            2: [lambda: pl.when(between)(lambda: on_side(1, t - 1, whole_block))],
            4: [lambda: pl.when((t > 2) | between)(lambda: on_side(0, t - 2, reduce_and_give))],
            5: [lambda: pl.when(t > 2)(lambda: on_side(1, t - 2, reduce_and_give))],
        })
        on(t, landed)
        return carry

    lax.fori_loop(2, hops, middle, 0)

    low, high = slice(0, hr), slice(hr, img_rows)

    def first_half(p, side):
        finish(cross(p, 0, low) + cross(p, 1, low), p, 0)

    def third_quarter(p, side):
        held[side] = cross(p, 0, high)

    def last_quarter(p, side):
        finish(held[side] + cross(p, 1, high), p, 1)

    if hops > 2:
        pl.when(tip)(lambda: on(hops - 1, whole_block))
    def first_product(p, side):
        full_held[...] = cross(p, 0, slice(0, img_rows))

    def second_product(p, side):
        full = full_held[...] + cross(p, 1, slice(0, img_rows))
        for h in range(2):
            finish(full[h * hr:(h + 1) * hr], p, h)

    def mid(act):
        return lambda: pl.when(between)(act)

    jobs = {
        1: [mid(lambda: on_side(0, hops - 1, first_product))],
        2: [mid(lambda: on_side(0, hops - 1, second_product))],
        3: [mid(lambda: on_side(1, hops - 1, first_product)),
            lambda: pl.when(tip)(lambda: on(hops, first_half))],
        4: [mid(lambda: on_side(1, hops - 1, second_product))],
        5: [lambda: pl.when(tip)(lambda: on(hops, third_quarter))],
        6: [lambda: pl.when(tip)(lambda: on(hops - 1, reduce_block))],
    }
    if hops == 2:
        jobs[0] = [mid(lambda: whole_block(z, 0))]
    run(hops, jobs)

    @pl.when(between)
    def _():
        on(hops, first_half)
        on(hops, third_quarter)

    on(hops, last_quarter)

    @pl.when(tip)
    def _():
        on(hops - 1, give_all)

    pl.when(between if hops == 2 else z >= 0)(lambda: on(hops - 2, reduce_and_give))

    @pl.when(between)
    def _():
        on(hops - 1, reduce_and_give)

    on(hops, functools.partial(reduce_block, last=True))
    on(hops, landed)
    on(hops, give_all)

    def combine(rows, at):
        m = rows[0][0:1, :]
        for row in rows[1:]:
            m = jnp.maximum(m, row[0:1, :])
        total = jnp.zeros_like(m)
        for row in rows:
            total = total + row[1:2, :] * jnp.exp(row[0:1, :] - m)
        y, b, p = at
        zstat[y, b, 0, pl.ds(p, 1), :] = m
        zstat[y, b, 1, pl.ds(p, 1), :] = total
        zstat[y, b, 2, pl.ds(p, 1), :] = rows[0][2:3, :]

    def stats(p):
        @pl.when(last_here != p)
        def _():
            drain(lstat.at[pl.ds(1, D * S - 1), p], st_send.at[p], st_recv.at[p]).wait_recv()
            for b in range(D):
                combine([lstat[b * S + k, p] for k in range(S)], (z, b, p))

        @pl.when(last_here == p)
        def _():
            for b in range(D):
                for row, value in enumerate((floor_value, 0.0, -2.0)):
                    zstat[z, b, row, pl.ds(p, 1), :] = jnp.full((1, img_rows), value, jnp.float32)

    if O > 8:
        lax.fori_loop(0, O, lambda p, carry: (stats(p), carry)[1], 0)
    else:
        for p in range(O):
            stats(p)

    def column(o):
        return pltpu.make_async_remote_copy(
            src_ref=zstat.at[z], dst_ref=zstat.at[z], send_sem=z_send, recv_sem=z_recv,
            device_id=dev(lax.rem(z + o, O), d, s), device_id_type=MESH)

    for o in range(1, O):
        column(o).start()

    def dom_wait(p, carry):
        @pl.when(used(p))
        def _():
            for od in range(1, D):
                across(od, p).wait_recv()
                keep_copy(lax.rem(d + D - od, D), p).start()
        return carry

    lax.fori_loop(0, O, dom_wait, 0)

    @pl.when(owner == d)
    def _():
        drain(erecv.at[pl.ds(1, S - 1)], e_send, e_recv).wait_recv()

    @pl.when(owner != d)
    def _():
        drain(erecv, e_send, e_recv).wait_recv()

    drain(zstat.at[pl.ds(1, O - 1)], z_send, z_recv).wait_recv()
    drain(zstat.at[pl.ds(1, O - 1)], z_send, z_recv).wait_send()

    @pl.when(member)
    def _():
        drain(fstat.at[pl.ds(1, len(lasts) * D * S - 1)], f_send, f_recv).wait_recv()
        for k in range(D * S):
            lstat[k, last_here] = fstat[rank * D * S + k]

    if len(lasts) < O:
        @pl.when(jnp.logical_not(member))
        def _():
            drain(fstat, f_send, f_recv).wait_recv()

    for i, (y, p) in enumerate(last_of.items()):
        for b in range(D):
            combine([fstat[(i * D + b) * S + k] for k in range(S)], (y, b, p))
    for b in range(D):
        def norm(j, carry, b=b):
            m_all, t_all, mine = zstat[:, b, 0], zstat[:, b, 1], zstat[:, b, 2] == jnp.asarray(j, jnp.float32)
            m = jnp.max(jnp.max(jnp.where(mine, m_all, floor_value), axis=0), axis=0, keepdims=True)
            total = jnp.where(mine, t_all * jnp.exp(jnp.where(mine, m_all - m, 0.0)), 0.0)
            total = jnp.sum(jnp.sum(total, axis=0), axis=0, keepdims=True)
            logn[b, j] = m + jnp.log(total)
            return carry

        if O > 8:
            lax.fori_loop(0, O, norm, 0)
        else:
            for j in range(O):
                norm(j, 0)

    pick = logn[d, 0]
    for j in range(1, O):
        pick = jnp.where(z == j, logn[d, j], pick)
    home_ref[...] = pick

    def posterior(b, q, p):
        k = d * per + q
        name = lstat[b * S + k, p, 2:3, :]
        whole = jnp.zeros_like(name)
        for j in range(max(p - skip, 0), min(p + skip, O - 1) + 1):
            whole = jnp.where(name == j, logn[b, j], whole)
        scale = jnp.exp(lstat[b * S + k, p, 0:1, :] - whole)
        return (erecv[b * per + q, p].astype(jnp.float32) * scale).astype(jnp.bfloat16)

    for q in range(per):
        for b in range(D):
            for p in range(0, O, 2):
                both = [posterior(b, q, i) for i in range(p, min(p + 2, O))]
                at = slice((b * O + p) * img_rows, (b * O + p + len(both)) * img_rows)
                prob_ref[q * lanes:(q + 1) * lanes, at] = jnp.concatenate(both, axis=1)

    def sent(p, carry):
        @pl.when(used(p))
        def _():
            for od in range(1, D):
                across(od, p).wait_send()
            drain(recvp.at[p], rs_send.at[p], rs_recv.at[p]).wait_send()

        @pl.when(last_here != p)
        def _():
            drain(lstat.at[pl.ds(1, D * S - 1), p], st_send.at[p], st_recv.at[p]).wait_send()

        for side, edge, before in ((0, O - 1, O - 2), (1, 0, 1)):
            beyond = p <= z if side == 0 else p >= z
            went = (z != edge) & beyond
            if skip:
                near_edge = (z == before) & ((p >= O - 1 - room) if side == 0 else (p <= room))
                went = went & ((z != before) | near_edge)

            @pl.when(went)
            def _():
                sem = up_sem if side == 0 else dn_sem
                drain(images.at[d, p], sem.at[p], img_sem.at[p, 0]).wait_send()
        return carry

    lax.fori_loop(0, O, sent, 0)
    @pl.when(owner == d)
    def _():
        drain(erecv.at[pl.ds(1, S - 1)], e_send, e_recv).wait_send()

    @pl.when(owner != d)
    def _():
        drain(erecv, e_send, e_recv).wait_send()

    @pl.when(member)
    def _():
        if len(lasts) == O:
            drain(fstat.at[pl.ds(1, O * D * S - 1)], f_send, f_recv).wait_send()
        else:
            for y in range(O - 1):
                drain(lstat.at[:, 0], f_send, f_recv).wait_send()
            drain(lstat.at[pl.ds(1, D * S - 1), 0], f_send, f_recv).wait_send()

    pltpu.make_async_copy(keep_ref, keep_ref, out_sem).wait()
    if skip:
        for side, edge in ((0, O - 1), (1, 0)):
            @pl.when(z == edge)
            def _():
                kept_copy(side).wait_send()


def product(prob_ref, home_ref, images, out_ref, logn_ref, total, out_sem):
    halves, width, wide = 2, images.shape[2], 1024

    def put(c, n):
        cols = pl.ds(n * wide, wide)
        return pltpu.make_async_copy(
            total.at[c, :, cols], out_ref.at[:, c, cols], out_sem.at[c, n])

    logn_ref[...] = home_ref[...]
    for c in range(halves):
        for n in range(width // wide):
            cols = slice(n * wide, (n + 1) * wide)
            total[c, :, cols] = jnp.dot(
                prob_ref[...], images[c, :, cols], preferred_element_type=jnp.float32)
            put(c, n).start()
    for c in range(halves):
        for n in range(width // wide):
            put(c, n).wait()


def grant(shapes):
    total = 6 * 1024 * 1024
    for item in shapes:
        if getattr(item, "memory_space", None) == pltpu.VMEM:
            size = jnp.dtype(item.dtype).itemsize
            *lead, tall, wide = item.shape
            tall, wide = -(-tall // 8) * 8, -(-wide // 128) * 128
            total += math.prod(lead) * tall * wide * size
    return total


def shards(references, images, noise_var, shell_of, kept_blocks):
    O, D, S = (lax.axis_size(a) for a in ("orient", "dom", "shell"))
    rows = references.shape[0]
    img_rows = images.shape[0]
    local = references.shape[2]
    flat = 2 * local
    lanes = rows // S
    own = rows // D
    columns = O * img_rows
    vmem = pl.BlockSpec(memory_space=pltpu.VMEM)
    sem = pltpu.SemaphoreType.DMA
    f32, bf16 = jnp.float32, jnp.bfloat16
    most = kept_blocks.shape[2]
    skip = max(O - most, 0)
    room = O - 1 - skip
    first = [
        pltpu.VMEM((D, O, 2, img_rows, local), bf16),
        pltpu.VMEM((2, room if skip else 1, 2, img_rows, local), bf16),
        pltpu.VMEM((most, 1, 128), f32),
        pltpu.VMEM((2, most, 1, 128), f32),
        pltpu.VMEM((2, O, 1, local), f32),
        pltpu.VMEM((O, S, img_rows, lanes), f32),
        pltpu.VMEM((O, S - 1, img_rows, lanes), f32),
        pltpu.VMEM((2, img_rows // 2, rows), f32),
        pltpu.VMEM((img_rows, rows), f32),
        pltpu.VMEM((rows, flat), bf16),
        pltpu.VMEM((rows, 2, local), bf16),
        pltpu.VMEM((img_rows, 2, local), bf16),
        pltpu.VMEM((O, lanes, img_rows), bf16),
        pltpu.VMEM((S, O, lanes, img_rows), bf16),
        pltpu.VMEM((D * S, O, 4, img_rows), f32),
        pltpu.VMEM((O, D, 3, O, img_rows), f32),
        pltpu.VMEM((len(farthest(O, most)) * D * S, 4, img_rows), f32),
        pltpu.VMEM((D, O, 1, img_rows), f32),
        pltpu.VMEM((1, local), f32),
        pltpu.VMEM((S, 1, lanes), f32),
        pltpu.VMEM((1, local), jnp.int32),
        pltpu.SMEM((most,), jnp.int32),
        pltpu.SMEM(noise_var.shape, f32),
        pltpu.SMEM((O,), jnp.int32),
        sem((O,)), sem((O,)), sem((O, 8)),
        sem((D - 1, O)), sem((D - 1, O)),
        sem((O,)), sem((O,)),
        sem((O,)), sem((O,)),
        sem, sem,
        sem, sem, sem((2,)), sem((2,)),
        sem, sem, sem, sem((5,)),
    ]
    probs, home, kept_images = pl.pallas_call(
        functools.partial(kernel, (O, D, S)),
        name="expectation",
        out_shape=(
            jax.ShapeDtypeStruct((own, D * columns), bf16),
            jax.ShapeDtypeStruct((1, img_rows), f32),
            jax.ShapeDtypeStruct((2, D, O, img_rows, local), bf16),
        ),
        in_specs=[pl.BlockSpec(memory_space=pltpu.HBM)] * 5,
        out_specs=(vmem, vmem, pl.BlockSpec(memory_space=pl.ANY)),
        scratch_shapes=first,
        compiler_params=pltpu.CompilerParams(collective_id=0, has_side_effects=True, vmem_limit_bytes=grant(first)),
    )(
        pltpu.with_memory_space_constraint(kept_blocks.reshape(-1), pltpu.HBM),
        pltpu.with_memory_space_constraint(noise_var, pltpu.HBM),
        pltpu.with_memory_space_constraint(shell_of.reshape(1,-1), pltpu.HBM),
        pltpu.with_memory_space_constraint(references, pltpu.HBM),
        pltpu.with_memory_space_constraint(images, pltpu.HBM),
    )
    depth = D * columns
    second = [
        pltpu.VMEM((2, own, local), f32),
        sem((2, local // 1024)),
    ]
    weighted, log_norm = pl.pallas_call(
        product,
        name="product",
        out_shape=(
            jax.ShapeDtypeStruct((own, 2, local), f32),
            jax.ShapeDtypeStruct((1, img_rows), f32),
        ),
        in_specs=[vmem, vmem, vmem],
        out_specs=(pl.BlockSpec(memory_space=pl.ANY), vmem),
        scratch_shapes=second,
        compiler_params=pltpu.CompilerParams(vmem_limit_bytes=grant(second)),
    )(probs, home, kept_images.reshape(2, depth, local))
    return weighted, log_norm.reshape(img_rows)


def solution(mesh):
    placed = (
        P("orient", None, "shell"),
        P(("orient", "dom"), None, "shell"),
        P(),
        P("shell"),
        P("orient", "dom", None),
    )
    return jax.shard_map(
        shards,
        mesh=mesh,
        in_specs=placed,
        out_specs=(P(("orient", "dom"), None, "shell"), P(("orient", "dom"))),
        check_vma=False,
    )
```

```python
import functools
import math

import jax
import jax.numpy as jnp
from jax import lax
from jax.experimental import pallas as pl
from jax.experimental.pallas import tpu as pltpu
from jax.sharding import PartitionSpec as P

floor_value = -1e30
MESH = pl.DeviceIdType.MESH


def farthest(O, most):
    skip = max(O - most, 0)
    room = O - 1 - skip
    hops = max(O - 2, room)
    found = {}
    for y in range(O):
        for p in (y - hops, y + hops):
            off = skip and ((y == O - 1 and p < skip) or (y == 0 and p > room))
            if 0 <= p < O and not off:
                found[y] = p
    return found


def kernel(
    sizes, kept_hbm, noise_hbm, shell_hbm, raw_ref, whole_ref, prob_ref, home_ref, keep_ref,
    images, slots, kout, kin, shift, part, recvp, held, full_held, refs_ref, stage, img_stage,
    ebuf, erecv, lstat, zstat, fstat, logn, w_s, rn_s, shell_ref, kept_ref, noise_ref, ids,
    up_sem, dn_sem, img_sem, dom_send, dom_recv, rs_send, rs_recv, st_send, st_recv,
    e_send, e_recv, z_send, z_recv, k_send, k_recv, f_send, f_recv, out_sem, in_sem,
):
    O, D, S = sizes
    z, d, s = lax.axis_index("orient"), lax.axis_index("dom"), lax.axis_index("shell")
    rows, _, half = raw_ref.shape
    img_rows = whole_ref.shape[0]
    lanes = rows // S
    per = S // D
    most = kept_ref.shape[0]
    owner = s // per
    slot = s % per
    skip = max(O - most, 0)
    room = O - 1 - skip
    hops = max(O - 2, room)
    pieces, chunks = 8, 8
    hr, qr, pr = img_rows // 2, img_rows // 4, rows // pieces

    def dev(a, b, c):
        return {"orient": a, "dom": b, "shell": c}

    inputs = [
        pltpu.make_async_copy(src, dst, in_sem.at[i])
        for i, (src, dst) in enumerate((
            (whole_ref, img_stage), (raw_ref, stage), (kept_hbm, kept_ref),
            (noise_hbm, noise_ref), (shell_hbm, shell_ref)))
    ]
    inputs[0].start()
    inputs[2].start()
    barrier = pltpu.get_barrier_semaphore()
    for ok, to in ((z < O - 1, z + 1), (z > 0, z + O - 1)):
        @pl.when(ok)
        def _():
            pl.semaphore_signal(
                barrier, inc=1, device_id=dev(lax.rem(to, O), d, s), device_id_type=MESH)

    for od in range(D):
        for os in range(S):
            if od or os:
                pl.semaphore_signal(
                    barrier, inc=1,
                    device_id=dev(z, lax.rem(d + od, D), lax.rem(s + os, S)),
                    device_id_type=MESH,
                )

    for i in (1, 3, 4):
        inputs[i].start()

    def used(p):
        if not skip:
            return p >= 0
        return jnp.logical_not(((z == O - 1) & (p < skip)) | ((z == 0) & (p > room)))

    def has(side, t):
        p = z - t if side == 0 else z + t
        inside = (p >= 0) & (p < O)
        return inside & used(p)

    def on(t, act):
        if isinstance(t, int) and t == 0:
            act(z, 0)
            return
        for side in range(2):
            @pl.when(has(side, t))
            def _():
                act(z - t if side == 0 else z + t, side)

    def piece(n):
        h, c, q = n // 4, (n // 2) % 2, n % 2
        return c, pl.ds(h * hr + q * qr, qr)

    def hop(side, src, p, n):
        c, at = piece(n)
        to = lax.rem(z + 1, O) if side == 0 else lax.rem(z + O - 1, O)
        send = up_sem if side == 0 else dn_sem
        return pltpu.make_async_remote_copy(
            src_ref=src.at[c, at], dst_ref=images.at[d, p, c, at], send_sem=send,
            recv_sem=img_sem.at[p - side, n], device_id=dev(to, d, s), device_id_type=MESH)

    def step(side, p, m):
        return p - m if side == 0 else p + m

    def choose(side, k, n):
        c, at = piece(n)
        first = step(side, z, k)
        v = images[d, first, c, at].astype(jnp.float32)

        def take(m, v):
            other = images[d, step(side, first, m), c, at].astype(jnp.float32)
            return jnp.where(shift[side, k + m] == m, other, v)

        v = lax.fori_loop(1, skip + 1, take, v, unroll=skip < 3)
        slots[side, k, c, at] = v.astype(jnp.bfloat16)

    def relay(side, t, n):
        p = step(side, z, t)
        edge = O - 1 if side == 0 else 0
        before = O - 2 if side == 0 else 1
        plain = (z != edge) & (z != before) if skip else z != edge

        @pl.when(plain)
        def _():
            hop(side, images.at[d, p], p, n).start()

        if skip and not (isinstance(t, int) and t < skip):
            k = t - skip

            @pl.when((z == before) & (k >= 0) & (k < room))
            def _():
                choose(side, k, n)
                hop(side, slots.at[side, k], step(side, z, k), n).start()

    def serve(t, n):
        def arrived(p, side):
            hop(side, images.at[d, p], p, n).wait_recv()
            relay(side, t, n)
        on(t, arrived)

    def across(od, p):
        return pltpu.make_async_remote_copy(
            src_ref=images.at[d, p], dst_ref=images.at[d, p],
            send_sem=dom_send.at[od - 1], recv_sem=dom_recv.at[od - 1, p],
            device_id=dev(z, lax.rem(d + od, D), s), device_id_type=MESH)

    def keep_copy(b, p):
        return pltpu.make_async_copy(images.at[b, p], keep_ref.at[:, b, p], out_sem)

    def landed(p, side):
        for od in range(1, D):
            across(od, p).start()
        keep_copy(d, p).start()

    def scatter(p, h, o):
        to = lax.rem(s + o, S)
        at = pl.ds(h * hr, hr)
        return pltpu.make_async_remote_copy(
            src_ref=part.at[p, to, at], dst_ref=recvp.at[p, o - 1, at], send_sem=rs_send,
            recv_sem=rs_recv.at[p], device_id=dev(z, d, to), device_id_type=MESH)

    peers = [(od, os) for od in range(D) for os in range(S) if od or os]

    def spread(p, od, os):
        return pltpu.make_async_remote_copy(
            src_ref=lstat.at[d * S + s, p], dst_ref=lstat.at[d * S + s, p],
            send_sem=st_send, recv_sem=st_recv.at[p],
            device_id=dev(z, lax.rem(d + od, D), lax.rem(s + os, S)), device_id_type=MESH)

    def give(p, to):
        return pltpu.make_async_remote_copy(
            src_ref=ebuf.at[p], dst_ref=erecv.at[d * per + slot, p], send_sem=e_send,
            recv_sem=e_recv, device_id=dev(z, owner, to), device_id_type=MESH)

    def give_all(p, side):
        for to in range(S):
            @pl.when((owner != d) | (s != to))
            def _():
                give(p, to).start()

    last_of = farthest(O, most)
    lasts = list(last_of)
    rank = sum(jnp.where(z == y, i, 0) for i, y in enumerate(lasts))
    member = functools.reduce(jnp.logical_or, [z == y for y in lasts])
    last_here = sum(jnp.where(z == y, p, 0) for y, p in last_of.items())
    last_here = jnp.where(member, last_here, -1)

    def everywhere():
        mine = (rank * D + d) * S + s
        for i in range(O):
            y = jnp.where(z < O // 2, O - 1 - i, i)
            for od, os in peers[::-1] + [(0, 0)]:
                copy = pltpu.make_async_remote_copy(
                    src_ref=fstat.at[mine], dst_ref=fstat.at[mine], send_sem=f_send,
                    recv_sem=f_recv,
                    device_id=dev(y, lax.rem(d + od, D), lax.rem(s + os, S)),
                    device_id_type=MESH)
                if od or os:
                    copy.start()
                else:
                    pl.when(y != z)(copy.start)

    def publish(p, m, total, name, e, last=False):
        mine = (rank * D + d) * S + s if last else d * S + s
        ref = fstat.at[mine] if last else lstat.at[mine, p]
        ref[0:1, :] = m
        ref[1:2, :] = total
        ref[2:3, :] = name
        ref[3:4, :] = jnp.zeros_like(m)
        if last:
            everywhere()
        else:
            for od, os in peers:
                spread(p, od, os).start()
        ebuf[p] = e

        @pl.when(owner == d)
        def _():
            erecv[d * per + slot, p] = e

    def drain(ref, send_sem, recv_sem):
        return pltpu.make_async_remote_copy(
            src_ref=ref, dst_ref=ref, send_sem=send_sem, recv_sem=recv_sem,
            device_id=dev(z, lax.rem(d + 1, D), s), device_id_type=MESH)

    def spread_rows(n):
        r0 = pl.multiple_of(n * pr, pr)
        x = stage[pl.ds(r0, pr)]
        refs_ref[pl.ds(r0, pr), :half] = x[:, 0, :]
        refs_ref[pl.ds(r0, pr), half:] = x[:, 1, :]

    def norm_rows(c):
        at = slice(c * lanes, (c + 1) * lanes)
        x0 = refs_ref[at, :half].astype(jnp.float32)
        x1 = refs_ref[at, half:].astype(jnp.float32)
        y = (x0 * x0 + x1 * x1) * w_s[...]
        acc = y[:, :128]
        for k in range(1, y.shape[1] // 128):
            acc = acc + y[:, k * 128:(k + 1) * 128]
        rn_s[c] = 0.5 * jnp.sum(acc.T, axis=0, keepdims=True)

    def cross(p, c, at):
        scaled = (images[d, p, c, at].astype(jnp.float32) * w_s[...]).astype(jnp.bfloat16)
        return lax.dot_general(
            scaled, refs_ref[:, c * half:(c + 1) * half], (((1,), (1,)), ((), ())),
            preferred_element_type=jnp.float32)

    def finish(full, p, h):
        at = pl.ds(h * hr, hr)
        for k in range(S):
            part[p, k, at] = full[:, k * lanes:(k + 1) * lanes] - rn_s[k]
        for o in sorted(range(1, S), key=lambda o: o % 2 == 0):
            scatter(p, h, o).start()

    def whole_block(p, side):
        every = slice(0, img_rows)
        full = cross(p, 0, every) + cross(p, 1, every)
        for h in range(2):
            finish(full[h * hr:(h + 1) * hr], p, h)

    def reduce_block(p, side, last=False):
        drain(recvp.at[p], rs_send, rs_recv.at[p]).wait_recv()
        v = part[p, s]
        for o in range(S - 1):
            v = v + recvp[p, o]
        v = v.T
        want = jnp.full(v.shape, ids[p], jnp.int32)
        keep = want == kept_ref[0]
        for k in range(1, most):
            keep = keep | (want == kept_ref[k])
        v = jnp.where(keep, v, floor_value)
        m = jnp.max(v, axis=0, keepdims=True)
        e = jnp.where(keep, jnp.exp(v - m), 0.0)
        total = jnp.sum(e, axis=0, keepdims=True)
        publish(p, m, total, want[:1].astype(jnp.float32), e.astype(jnp.bfloat16), last)

    def kept_copy(side):
        to = lax.rem(z + O - 1, O) if side == 0 else lax.rem(z + 1, O)
        return pltpu.make_async_remote_copy(
            src_ref=kout, dst_ref=kin.at[side], send_sem=k_send,
            recv_sem=k_recv.at[side], device_id=dev(to, d, s), device_id_type=MESH)

    def own_rows(h):
        at = slice(h * hr, (h + 1) * hr)
        x = img_stage[at]
        for c in range(2):
            images[d, z, c, at] = x[:, c, :]

    between = (z > 0) & (z < O - 1)
    tip = jnp.logical_not(between)
    inputs[2].wait()
    if skip:
        @pl.when(tip)
        def _():
            for k in range(most):
                kout[k] = jnp.full((1, 128), kept_ref[k], jnp.int32).astype(jnp.float32)
    inputs[0].wait()
    own_rows(0)
    near = jnp.where(z < O - 1, 1, 0) + jnp.where(z > 0, 1, 0)
    pl.semaphore_wait(barrier, near + D * S - 1)
    if skip:
        for side, last in ((0, O - 1), (1, 0)):
            @pl.when(z == last)
            def _():
                kept_copy(side).start()
    for h in range(2):
        if h:
            own_rows(h)
        for n in range(4 * h, 4 * h + 4):
            for side in range(2):
                relay(side, 0, n)
    landed(z, 0)
    inputs[1].wait()

    def candidate(side, c):
        return O - 2 - c if side == 0 else 1 + c

    for p in range(O):
        ids[p] = p
    if skip:
        for side, edge in ((0, O - 1), (1, 0)):
            @pl.when(z == edge)
            def _():
                gone, moved = jnp.int32(0), []
                for c in range(O - 1):
                    moved.append(jnp.minimum(gone, skip))
                    need = kept_ref[0] == candidate(side, c)
                    for k in range(1, most):
                        need = need | (kept_ref[k] == candidate(side, c))
                    gone = gone + jnp.where(need, 0, 1)
                for k in range(room):
                    name = jnp.int32(candidate(side, k))
                    for m in range(1, skip + 1):
                        name = jnp.where(moved[k + m] == m, candidate(side, k + m), name)
                    ids[candidate(side, k)] = name
                for k in range(room, O - 1):
                    p = candidate(side, k)
                    for b in range(D):
                        images[b, p] = jnp.zeros((2, img_rows, half), jnp.bfloat16)
                        keep_copy(b, p).start()
                    publish(
                        p, jnp.full((1, img_rows), floor_value, jnp.float32),
                        jnp.zeros((1, img_rows), jnp.float32),
                        jnp.full((1, img_rows), -2.0, jnp.float32),
                        jnp.zeros((lanes, img_rows), jnp.bfloat16))
                    give_all(p, 0)

    def shifts():
        for side, before in ((0, O - 2), (1, 1)) if skip else ():
            @pl.when(z == before)
            def _():
                kept_copy(side).wait_recv()
                gone = jnp.zeros((1, 128), jnp.float32)
                for c in range(O - 1):
                    moved = jnp.minimum(gone, skip)
                    shift[side, c] = jnp.concatenate([moved] * (half // 128), axis=1)
                    need = jnp.zeros((1, 128), jnp.float32)
                    for k in range(most):
                        need = jnp.where(kin[side, k] == candidate(side, c), 1.0, need)
                    gone = gone + 1.0 - need

    def weights():
        inputs[3].wait()
        inputs[4].wait()
        shell = shell_ref[...]
        noise = jnp.ones(shell.shape, jnp.float32)
        for i in range(noise_ref.shape[0]):
            noise = jnp.where(shell == i, noise_ref[i], noise)
        w_s[...] = 1.0 / noise

    def on_side(side, t, act):
        @pl.when(has(side, t))
        def _():
            act(step(side, z, t), side)

    def reduce_and_give(p, side):
        reduce_block(p, side)
        give_all(p, side)

    def run(t, jobs):
        for n in range(chunks):
            serve(t, n)
            for job in jobs.get(n, ()):
                job()

    @pl.when(tip)
    def _():
        for n in range(pieces):
            spread_rows(n)
        weights()
        for c in range(S):
            norm_rows(c)
        whole_block(z, 0)
        run(1, {})
        on(1, whole_block)
        on(1, landed)
        reduce_and_give(z, 0)

    @pl.when(between)
    def _():
        for n in range(3):
            spread_rows(n)
        shifts()
        jobs = {n: [functools.partial(spread_rows, n + 3)] for n in range(pieces - 3)}
        norms = [functools.partial(norm_rows, c) for c in range(S)]
        jobs[5] = [weights] + norms[:S // 2]
        jobs[6] = norms[S // 2:]
        run(1, jobs)
        on(1, landed)

    def middle(t, carry):
        pl.when(tip & (t > 2))(lambda: on(t - 1, whole_block))
        pl.when(between & (t == 2))(lambda: whole_block(z, 0))
        run(t, {
            0: [lambda: pl.when(between)(lambda: on_side(0, t - 1, whole_block))],
            2: [lambda: pl.when(between)(lambda: on_side(1, t - 1, whole_block))],
            4: [lambda: pl.when((t > 2) | between)(lambda: on_side(0, t - 2, reduce_and_give))],
            5: [lambda: pl.when(t > 2)(lambda: on_side(1, t - 2, reduce_and_give))],
        })
        on(t, landed)
        return carry

    lax.fori_loop(2, hops, middle, 0)

    low, high = slice(0, hr), slice(hr, img_rows)

    def first_half(p, side):
        finish(cross(p, 0, low) + cross(p, 1, low), p, 0)

    def third_quarter(p, side):
        held[side] = cross(p, 0, high)

    def last_quarter(p, side):
        finish(held[side] + cross(p, 1, high), p, 1)

    if hops > 2:
        pl.when(tip)(lambda: on(hops - 1, whole_block))
    def first_product(p, side):
        full_held[...] = cross(p, 0, slice(0, img_rows))

    def second_product(p, side):
        full = full_held[...] + cross(p, 1, slice(0, img_rows))
        for h in range(2):
            finish(full[h * hr:(h + 1) * hr], p, h)

    def mid(act):
        return lambda: pl.when(between)(act)

    jobs = {
        1: [mid(lambda: on_side(0, hops - 1, first_product))],
        2: [mid(lambda: on_side(0, hops - 1, second_product))],
        3: [mid(lambda: on_side(1, hops - 1, first_product)),
            lambda: pl.when(tip)(lambda: on(hops, first_half))],
        4: [mid(lambda: on_side(1, hops - 1, second_product))],
        5: [lambda: pl.when(tip)(lambda: on(hops, third_quarter))],
        6: [lambda: pl.when(tip)(lambda: on(hops - 1, reduce_block))],
    }
    if hops == 2:
        jobs[0] = [mid(lambda: whole_block(z, 0))]
    run(hops, jobs)

    @pl.when(between)
    def _():
        on(hops, first_half)
        on(hops, third_quarter)

    on(hops, last_quarter)

    @pl.when(tip)
    def _():
        on(hops - 1, give_all)

    pl.when(between if hops == 2 else z >= 0)(lambda: on(hops - 2, reduce_and_give))

    @pl.when(between)
    def _():
        on(hops - 1, reduce_and_give)

    on(hops, functools.partial(reduce_block, last=True))
    on(hops, landed)
    on(hops, give_all)

    def combine(rows, at):
        m = rows[0][0:1, :]
        for row in rows[1:]:
            m = jnp.maximum(m, row[0:1, :])
        total = jnp.zeros_like(m)
        for row in rows:
            total = total + row[1:2, :] * jnp.exp(row[0:1, :] - m)
        y, b, p = at
        zstat[y, b, 0, pl.ds(p, 1), :] = m
        zstat[y, b, 1, pl.ds(p, 1), :] = total
        zstat[y, b, 2, pl.ds(p, 1), :] = rows[0][2:3, :]

    def stats(p):
        @pl.when(last_here != p)
        def _():
            drain(lstat.at[pl.ds(1, D * S - 1), p], st_send, st_recv.at[p]).wait_recv()
            for b in range(D):
                combine([lstat[b * S + k, p] for k in range(S)], (z, b, p))

        @pl.when(last_here == p)
        def _():
            for b in range(D):
                for row, value in enumerate((floor_value, 0.0, -2.0)):
                    zstat[z, b, row, pl.ds(p, 1), :] = jnp.full((1, img_rows), value, jnp.float32)

    if O > 8:
        lax.fori_loop(0, O, lambda p, carry: (stats(p), carry)[1], 0)
    else:
        for p in range(O):
            stats(p)

    def column(o):
        return pltpu.make_async_remote_copy(
            src_ref=zstat.at[z], dst_ref=zstat.at[z], send_sem=z_send, recv_sem=z_recv,
            device_id=dev(lax.rem(z + o, O), d, s), device_id_type=MESH)

    for o in range(1, O):
        column(o).start()

    def dom_wait(p, carry):
        @pl.when(used(p))
        def _():
            for od in range(1, D):
                across(od, p).wait_recv()
                keep_copy(lax.rem(d + D - od, D), p).start()
        return carry

    lax.fori_loop(0, O, dom_wait, 0)

    @pl.when(owner == d)
    def _():
        drain(erecv.at[pl.ds(1, S - 1)], e_send, e_recv).wait_recv()

    @pl.when(owner != d)
    def _():
        drain(erecv, e_send, e_recv).wait_recv()

    drain(zstat.at[pl.ds(1, O - 1)], z_send, z_recv).wait_recv()
    drain(zstat.at[pl.ds(1, O - 1)], z_send, z_recv).wait_send()

    @pl.when(member)
    def _():
        drain(fstat.at[pl.ds(1, len(lasts) * D * S - 1)], f_send, f_recv).wait_recv()
        for k in range(D * S):
            lstat[k, last_here] = fstat[rank * D * S + k]

    if len(lasts) < O:
        @pl.when(jnp.logical_not(member))
        def _():
            drain(fstat, f_send, f_recv).wait_recv()

    for i, (y, p) in enumerate(last_of.items()):
        for b in range(D):
            combine([fstat[(i * D + b) * S + k] for k in range(S)], (y, b, p))
    for b in range(D):
        def norm(j, carry, b=b):
            m_all, t_all, mine = zstat[:, b, 0], zstat[:, b, 1], zstat[:, b, 2] == jnp.asarray(j, jnp.float32)
            m = jnp.max(jnp.max(jnp.where(mine, m_all, floor_value), axis=0), axis=0, keepdims=True)
            total = jnp.where(mine, t_all * jnp.exp(jnp.where(mine, m_all - m, 0.0)), 0.0)
            total = jnp.sum(jnp.sum(total, axis=0), axis=0, keepdims=True)
            logn[b, j] = m + jnp.log(total)
            return carry

        if O > 8:
            lax.fori_loop(0, O, norm, 0)
        else:
            for j in range(O):
                norm(j, 0)

    pick = logn[d, 0]
    for j in range(1, O):
        pick = jnp.where(z == j, logn[d, j], pick)
    home_ref[...] = pick

    def posterior(b, q, p):
        k = d * per + q
        name = lstat[b * S + k, p, 2:3, :]
        whole = jnp.zeros_like(name)
        for j in range(max(p - skip, 0), min(p + skip, O - 1) + 1):
            whole = jnp.where(name == j, logn[b, j], whole)
        scale = jnp.exp(lstat[b * S + k, p, 0:1, :] - whole)
        return (erecv[b * per + q, p].astype(jnp.float32) * scale).astype(jnp.bfloat16)

    for q in range(per):
        for b in range(D):
            for p in range(0, O, 2):
                both = [posterior(b, q, i) for i in range(p, min(p + 2, O))]
                at = slice((b * O + p) * img_rows, (b * O + p + len(both)) * img_rows)
                prob_ref[q * lanes:(q + 1) * lanes, at] = jnp.concatenate(both, axis=1)

    def sent(blocks):
        for od in range(1, D):
            drain(images.at[d, pl.ds(0, blocks)], dom_send.at[od - 1], dom_recv.at[0, 0]).wait_send()
        drain(recvp.at[pl.ds(0, blocks)], rs_send, rs_recv.at[0]).wait_send()

    pl.when(between)(lambda: sent(O))
    pl.when(tip)(lambda: sent(room + 1))

    def told(blocks):
        every = lstat.at[pl.ds(1, D * S - 1), pl.ds(0, blocks)]
        drain(every, st_send, st_recv.at[0]).wait_send()

    pl.when(member)(lambda: told(O - 1))
    if len(lasts) < O:
        pl.when(jnp.logical_not(member))(lambda: told(O))

    def passed(side, blocks):
        sem = up_sem if side == 0 else dn_sem
        drain(images.at[d, pl.ds(0, blocks)], sem, img_sem.at[0, 0]).wait_send()

    for y in range(O):
        for side in range(2):
            ahead = y if side == 0 else O - 1 - y
            if ahead < O - 1:
                count = room if skip and ahead == O - 2 else ahead + 1
                pl.when(z == y)(functools.partial(passed, side, count))

    @pl.when(owner == d)
    def _():
        drain(erecv.at[pl.ds(1, S - 1)], e_send, e_recv).wait_send()

    @pl.when(owner != d)
    def _():
        drain(erecv, e_send, e_recv).wait_send()

    @pl.when(member)
    def _():
        if len(lasts) == O:
            drain(fstat.at[pl.ds(1, O * D * S - 1)], f_send, f_recv).wait_send()
        else:
            for y in range(O - 1):
                drain(lstat.at[:, 0], f_send, f_recv).wait_send()
            drain(lstat.at[pl.ds(1, D * S - 1), 0], f_send, f_recv).wait_send()

    pltpu.make_async_copy(keep_ref, keep_ref, out_sem).wait()
    if skip:
        for side, edge in ((0, O - 1), (1, 0)):
            @pl.when(z == edge)
            def _():
                kept_copy(side).wait_send()


def product(prob_ref, home_ref, images, out_ref, logn_ref, total, out_sem):
    halves, width, wide = 2, images.shape[2], 1024

    def put(c, n):
        cols = pl.ds(n * wide, wide)
        return pltpu.make_async_copy(
            total.at[c, :, cols], out_ref.at[:, c, cols], out_sem.at[c, n])

    logn_ref[...] = home_ref[...]
    for c in range(halves):
        for n in range(width // wide):
            cols = slice(n * wide, (n + 1) * wide)
            total[c, :, cols] = jnp.dot(
                prob_ref[...], images[c, :, cols], preferred_element_type=jnp.float32)
            put(c, n).start()
    for c in range(halves):
        for n in range(width // wide):
            put(c, n).wait()


def grant(shapes):
    total = 6 * 1024 * 1024
    for item in shapes:
        if getattr(item, "memory_space", None) == pltpu.VMEM:
            size = jnp.dtype(item.dtype).itemsize
            *lead, tall, wide = item.shape
            tall, wide = -(-tall // 8) * 8, -(-wide // 128) * 128
            total += math.prod(lead) * tall * wide * size
    return total


def shards(references, images, noise_var, shell_of, kept_blocks):
    O, D, S = (lax.axis_size(a) for a in ("orient", "dom", "shell"))
    rows = references.shape[0]
    img_rows = images.shape[0]
    local = references.shape[2]
    flat = 2 * local
    lanes = rows // S
    own = rows // D
    columns = O * img_rows
    vmem = pl.BlockSpec(memory_space=pltpu.VMEM)
    sem = pltpu.SemaphoreType.DMA
    f32, bf16 = jnp.float32, jnp.bfloat16
    most = kept_blocks.shape[2]
    skip = max(O - most, 0)
    room = O - 1 - skip
    first = [
        pltpu.VMEM((D, O, 2, img_rows, local), bf16),
        pltpu.VMEM((2, room if skip else 1, 2, img_rows, local), bf16),
        pltpu.VMEM((most, 1, 128), f32),
        pltpu.VMEM((2, most, 1, 128), f32),
        pltpu.VMEM((2, O, 1, local), f32),
        pltpu.VMEM((O, S, img_rows, lanes), f32),
        pltpu.VMEM((O, S - 1, img_rows, lanes), f32),
        pltpu.VMEM((2, img_rows // 2, rows), f32),
        pltpu.VMEM((img_rows, rows), f32),
        pltpu.VMEM((rows, flat), bf16),
        pltpu.VMEM((rows, 2, local), bf16),
        pltpu.VMEM((img_rows, 2, local), bf16),
        pltpu.VMEM((O, lanes, img_rows), bf16),
        pltpu.VMEM((S, O, lanes, img_rows), bf16),
        pltpu.VMEM((D * S, O, 4, img_rows), f32),
        pltpu.VMEM((O, D, 3, O, img_rows), f32),
        pltpu.VMEM((len(farthest(O, most)) * D * S, 4, img_rows), f32),
        pltpu.VMEM((D, O, 1, img_rows), f32),
        pltpu.VMEM((1, local), f32),
        pltpu.VMEM((S, 1, lanes), f32),
        pltpu.VMEM((1, local), jnp.int32),
        pltpu.SMEM((most,), jnp.int32),
        pltpu.SMEM(noise_var.shape, f32),
        pltpu.SMEM((O,), jnp.int32),
        sem, sem, sem((O - 1, 8)),
        sem((D - 1,)), sem((D - 1, O)),
        sem, sem((O,)),
        sem, sem((O,)),
        sem, sem,
        sem, sem, sem, sem((2,)),
        sem, sem, sem, sem((5,)),
    ]
    probs, home, kept_images = pl.pallas_call(
        functools.partial(kernel, (O, D, S)),
        name="expectation",
        out_shape=(
            jax.ShapeDtypeStruct((own, D * columns), bf16),
            jax.ShapeDtypeStruct((1, img_rows), f32),
            jax.ShapeDtypeStruct((2, D, O, img_rows, local), bf16),
        ),
        in_specs=[pl.BlockSpec(memory_space=pltpu.HBM)] * 5,
        out_specs=(vmem, vmem, pl.BlockSpec(memory_space=pl.ANY)),
        scratch_shapes=first,
        compiler_params=pltpu.CompilerParams(collective_id=0, has_side_effects=True, vmem_limit_bytes=grant(first)),
    )(
        pltpu.with_memory_space_constraint(kept_blocks.reshape(-1), pltpu.HBM),
        pltpu.with_memory_space_constraint(noise_var, pltpu.HBM),
        pltpu.with_memory_space_constraint(shell_of.reshape(1,-1), pltpu.HBM),
        pltpu.with_memory_space_constraint(references, pltpu.HBM),
        pltpu.with_memory_space_constraint(images, pltpu.HBM),
    )
    depth = D * columns
    second = [
        pltpu.VMEM((2, own, local), f32),
        sem((2, local // 1024)),
    ]
    weighted, log_norm = pl.pallas_call(
        product,
        name="product",
        out_shape=(
            jax.ShapeDtypeStruct((own, 2, local), f32),
            jax.ShapeDtypeStruct((1, img_rows), f32),
        ),
        in_specs=[vmem, vmem, vmem],
        out_specs=(pl.BlockSpec(memory_space=pl.ANY), vmem),
        scratch_shapes=second,
        compiler_params=pltpu.CompilerParams(vmem_limit_bytes=grant(second)),
    )(probs, home, kept_images.reshape(2, depth, local))
    return weighted, log_norm.reshape(img_rows)


def solution(mesh):
    placed = (
        P("orient", None, "shell"),
        P(("orient", "dom"), None, "shell"),
        P(),
        P("shell"),
        P("orient", "dom", None),
    )
    return jax.shard_map(
        shards,
        mesh=mesh,
        in_specs=placed,
        out_specs=(P(("orient", "dom"), None, "shell"), P(("orient", "dom"))),
        check_vma=False,
    )
```
